32 devices in a mesh: gx: 8 (over y, x, core), gy: 4 (over z).
Axes of the slice: x: 2, y: 2, z: 4, core: 2. Of those that a mesh axis runs over, the one named last changes fastest.
Arguments:
- pressure_now: float32 [64, 384, 768], P('gx', 'gy'), may hold values from -6 to 6
- pressure_prev: float32 [64, 384, 768], P('gx', 'gy'), may hold values from -6 to 6
- wave_speed: bfloat16 [64, 384, 768], P('gx', 'gy'), may hold values from 0.099609375 to 0.328125
- node_cell: int32 [8, 4, 2048], P('gx', 'gy'), may hold values from 0 to 589823, as said below
- node_material: int32 [8, 4, 2048], P('gx', 'gy'), may hold values from 0 to 7
- filter_state: float32 [8, 4, 2048], P('gx', 'gy'), may hold values from -6 to 6
- material_pole: float32 [8], replicated, may hold values from 0.3 to 0.95
- material_loss: float32 [8], replicated, may hold values from 0.1 to 0.6
- sphere_anchor: int32 [128, 3], replicated, may hold values from 0 to 720, as said below
Outputs:
- pressure: float32 [64, 384, 768], P('gx', 'gy')
- pressure_before: float32 [64, 384, 768], P('gx', 'gy')
- filter_out: float32 [8, 4, 2048], P('gx', 'gy')
- coefficients: float32 [128, 256], P('gy')
The draws below stay inside these ranges and needn't reach their ends.
Inputs may be any that keep to these rules, and one draw needn't show every extreme that they name: `node_cell`: within one device the node cells are distinct, and none lies in the outermost layer of cells of the device's block along the first or the second dimension. `sphere_anchor`: sphere s lies in the block row s // 32 along the second dimension: its y start is that row's first cell plus a multiple of 48; its z start is a multiple of 48; its x start is at most 16; spheres are placed unevenly along x and may intersect.
All inputs are finite; a program needn't handle non-finite values.
Results may differ from the reference program's by a relative error of at most 0.0019.
Values may be sent and summed in bfloat16 or wider, within the bound.
No kernel may reach another device: no remote copies, remote signals or barrier semaphores. Data moves between devices by JAX's collectives and lax.ppermute only.
A program may use at most 192 MiB of HBM per device.

```python
import math
import jax
import jax.numpy as jnp
import numpy as np
from jax import lax

CX = 8
CY = 96
NZ = 768
NB = 2048
NS = 128
CUBE = 48
COEFS = 256
MATS = 8
STEPS = 2
SLABS = 8
YPARTS = 4
NX = 64
NY = 384
SPR = 32


def draw_node_cell(key, part):
    interior = (CX - 2) * (CY - 2) * NZ
    stride = interior // NB
    offsets = jax.random.randint(key, (SLABS, YPARTS, NB), 0, stride)
    position = jnp.arange(NB, dtype=jnp.int32)[None, None, :] * stride + offsets
    z_cell = position % NZ
    y_cell = position // NZ % (CY - 2) + 1
    x_cell = position // (NZ * (CY - 2)) + 1
    return ((x_cell * CY + y_cell) * NZ + z_cell).astype(jnp.int32)


def draw_sphere_anchor(key, part):
    subkeys = jax.random.split(key, 5)
    hotspot = jax.random.randint(subkeys[0], (4,), 0, NX - CUBE + 1)
    chosen = jax.random.randint(subkeys[1], (NS,), 0, 4)
    jitter = jax.random.randint(subkeys[2], (NS,), -2 * CUBE, 2 * CUBE + 1)
    x_start = jnp.clip(hotspot[chosen] + jitter, 0, NX - CUBE)
    sphere_ids = jnp.arange(NS, dtype=jnp.int32)
    x_start = jnp.where(sphere_ids % SPR == 1, 0, x_start)
    row_index = sphere_ids // SPR
    y_start = row_index * CY + CUBE * jax.random.randint(subkeys[3], (NS,), 0, CY // CUBE)
    z_start = CUBE * jax.random.randint(subkeys[4], (NS,), 0, NZ // CUBE)
    return jnp.stack([x_start, y_start, z_start], axis=1).astype(jnp.int32)


def place_ends(values, stream_key, least, high):
    extent = values.shape
    index_at = [jax.random.randint(jax.random.fold_in(stream_key, axis), (), 0, extent[axis]) for axis in range(len(extent))]
    values = values.at[tuple(index_at)].set(least)
    longest = extent.index(max(extent))
    index_at[longest] = (index_at[longest] + 1) % extent[longest]
    return values.at[tuple(index_at)].set(high)


def steps_of(key, extent, cuts, smallest, high):
    def one(dim, parts):
        draws = jax.random.uniform(jax.random.fold_in(jax.random.fold_in(key, 6), dim), (parts,), jnp.float32, smallest / len(cuts), high / len(cuts))
        return jnp.repeat(jnp.exp(draws), extent[dim] // parts).reshape((-1,) + (1,) * (len(extent) - dim - 1))

    loudness = one(*cuts[0])
    for cut in cuts[1:]:
        loudness = loudness * one(*cut)
    return loudness


def gaussian(rng, shape, scale, reach, pieces=(), kind=jnp.bfloat16):
    array = scale * jax.random.normal(rng, shape, jnp.float32)
    if pieces:
        array = array * steps_of(rng, shape, pieces, -0.22, 0.18)
    return jnp.clip(array, -reach, reach).astype(kind)


def setup_inputs(seed: int = 0) -> dict:
    splits = jax.random.split(jax.random.key(seed), 10)
    return {
        "pressure_now": gaussian(splits[0], (NX, NY, NZ), 1.0, 6.0, ((0, 8), (1, 4)), jnp.float32),
        "pressure_prev": gaussian(splits[1], (NX, NY, NZ), 1.0, 6.0, ((0, 8), (1, 4)), jnp.float32),
        "wave_speed": jnp.clip(0.099609375 + 0.22851562 * jax.random.uniform(splits[2], (NX, NY, NZ), jnp.float32) ** steps_of(splits[2], (NX, NY, NZ), ((0, 8), (1, 4)), -0.2, 0.2), 0.099609375, 0.328125).astype(jnp.bfloat16),
        "node_cell": draw_node_cell(jax.random.fold_in(splits[9], 71), 0),
        "node_material": place_ends(jax.random.randint(splits[4], (SLABS, YPARTS, NB), 0, MATS), jax.random.fold_in(splits[4], 1), 0, MATS - 1).astype(jnp.int32),
        "filter_state": gaussian(splits[5], (SLABS, YPARTS, NB), 1.0, 6.0, ((0, 8), (1, 4)), jnp.float32),
        "material_pole": jnp.clip(jax.random.uniform(splits[6], (MATS,), jnp.float32, 0.3, 0.95), 0.3, 0.95),
        "material_loss": jnp.clip(jax.random.uniform(splits[7], (MATS,), jnp.float32, 0.1, 0.6), 0.1, 0.6),
        "sphere_anchor": draw_sphere_anchor(jax.random.fold_in(splits[9], 71), 0),
    }


def harmonic_table():
    half_side = CUBE / 2.0
    coords = (np.arange(CUBE) + 0.5 - half_side) / half_side
    x_pos, y_pos, z_pos = np.meshgrid(coords, coords, coords, indexing='ij')
    x_pos = x_pos.reshape(-1)
    y_pos = y_pos.reshape(-1)
    z_pos = z_pos.reshape(-1)
    radius_sq = x_pos * x_pos + y_pos * y_pos + z_pos * z_pos
    inside = np.where(radius_sq <= 1.0, 1.0, 0.0)
    degree_top = math.isqrt(COEFS) - 1
    zero_field = x_pos * 0.0
    real_part = {(0, 0): zero_field + 1.0}
    imag_part = {(0, 0): zero_field}
    for azimuth in range(1, degree_top + 1):
        last_real = real_part[azimuth - 1, azimuth - 1]
        last_imag = imag_part[azimuth - 1, azimuth - 1]
        real_part[azimuth, azimuth] = -(x_pos * last_real - y_pos * last_imag) / (2.0 * azimuth)
        imag_part[azimuth, azimuth] = -(x_pos * last_imag + y_pos * last_real) / (2.0 * azimuth)
    for azimuth in range(degree_top + 1):
        for degree in range(azimuth + 1, degree_top + 1):
            lower_real = real_part.get((degree - 2, azimuth), zero_field)
            lower_imag = imag_part.get((degree - 2, azimuth), zero_field)
            denom = float((degree - azimuth) * (degree + azimuth))
            real_part[degree, azimuth] = ((2 * degree - 1) * z_pos * real_part[degree - 1, azimuth] - radius_sq * lower_real) / denom
            imag_part[degree, azimuth] = ((2 * degree - 1) * z_pos * imag_part[degree - 1, azimuth] - radius_sq * lower_imag) / denom
    rows_list = []
    for degree in range(degree_top + 1):
        for azimuth in range(degree + 1):
            rows_list.append(real_part[degree, azimuth])
            if azimuth > 0:
                rows_list.append(imag_part[degree, azimuth])
    stacked = np.stack(rows_list) * inside[None, :]
    row_norms = np.sqrt(np.sum(stacked * stacked, axis=1, keepdims=True))
    return (stacked / row_norms).astype(np.float32)

def leapfrog(current, previous, wave_speed):
    padded = jnp.pad(current, 1)
    beside = padded[2:, 1:-1, 1:-1] + padded[:-2, 1:-1, 1:-1]
    beside = beside + padded[1:-1, 2:, 1:-1] + padded[1:-1, :-2, 1:-1]
    beside = beside + padded[1:-1, 1:-1, 2:] + padded[1:-1, 1:-1, :-2]
    return 2.0 * current - previous + wave_speed.astype(jnp.float32) * (beside - 6.0 * current)

def reference(pressure_now, pressure_prev, wave_speed, node_cell, node_material, filter_state, material_pole, material_loss, sphere_anchor):
    slab_ids = jnp.arange(SLABS, dtype=jnp.int32)[:, None, None]
    part_ids = jnp.arange(YPARTS, dtype=jnp.int32)[None, :, None]
    x_cell = slab_ids * CX + node_cell // (CY * NZ)
    y_cell = part_ids * CY + node_cell // NZ % CY
    z_cell = node_cell % NZ
    global_cell = ((x_cell * NY + y_cell) * NZ + z_cell).reshape(-1).astype(jnp.int32)
    pole_rate = material_pole[node_material].reshape(-1)
    loss_rate = material_loss[node_material].reshape(-1)
    filter_now = filter_state.reshape(-1)
    current, previous = (pressure_now, pressure_prev)
    for step in range(STEPS):
        advanced = leapfrog(current, previous, wave_speed)
        flattened = advanced.reshape(-1)
        filter_now = pole_rate * filter_now + (1.0 - pole_rate) * flattened[global_cell]
        flattened = flattened.at[global_cell].add(-loss_rate * filter_now)
        previous, current = (current, flattened.reshape(current.shape))
    probe_field = current.astype(jnp.bfloat16)
    harmonics = jnp.asarray(harmonic_table(), dtype=jnp.float32).astype(jnp.bfloat16)

    def extract(anchor):
        return lax.dynamic_slice(probe_field, (anchor[0], anchor[1], anchor[2]), (CUBE, CUBE, CUBE)).reshape(-1)
    patches = jax.vmap(extract)(sphere_anchor)
    coefficients = lax.dot_general(patches.astype(jnp.float32), harmonics.astype(jnp.float32), (((1,), (1,)), ((), ())), preferred_element_type=jnp.float32)
    return (current, previous, filter_now.reshape(filter_state.shape), coefficients)
```

```python
import functools
import math

import jax
import jax.numpy as jnp
import ml_dtypes
import numpy as np
from jax import lax
from jax.experimental import pallas as pl
from jax.experimental.pallas import tpu as pltpu
from jax.sharding import PartitionSpec as P

CUBE = 48
COEFS = 256
DEGREES = 16
LANES = 128
GROUP = 128
F32 = jnp.float32
BF16 = jnp.bfloat16


def halves(table):
    high = table.astype(ml_dtypes.bfloat16)
    low = (table - high.astype(np.float64)).astype(ml_dtypes.bfloat16)
    return high, low


@functools.lru_cache(maxsize=None)
def tables():
    axis = (np.arange(CUBE) + 0.5 - CUBE / 2.0) / (CUBE / 2.0)
    u, v = np.meshgrid(axis, axis, indexing="ij")
    planar_index, planar = {}, []
    for degree in range(DEGREES):
        for m in range(degree % 2, degree + 1, 2):
            k = (degree - m) // 2
            value = (-(u + 1j * v)) ** m * (u * u + v * v) ** k
            for part in range(2 if m else 1):
                planar_index[m, k, part] = len(planar)
                planar.append(value.imag if part else value.real)
    planar = np.stack(planar)
    axial = np.stack([axis**q for q in range(DEGREES)])
    poly = {}
    for m in range(DEGREES):
        poly[m, m] = {0: 1.0}
        for n in range(m + 1, DEGREES):
            entry = {}
            for k, c in poly[n - 1, m].items():
                entry[k] = entry.get(k, 0.0) + (2 * n - 1) * c
            for k, c in poly.get((n - 2, m), {}).items():
                entry[k] = entry.get(k, 0.0) - c
                entry[k + 1] = entry.get(k + 1, 0.0) - c
            poly[n, m] = {k: c / ((n - m) * (n + m)) for k, c in entry.items()}
    mix = np.zeros((DEGREES, len(planar), COEFS))
    row = 0
    for n in range(DEGREES):
        for m in range(n + 1):
            for part in range(2 if m else 1):
                for k, c in poly[n, m].items():
                    mix[n - m - 2 * k, planar_index[m, k, part], row] = c
                row += 1
    ball = (
        axis[:, None, None] ** 2 + axis[None, :, None] ** 2 + axis[None, None, :] ** 2
    ) <= 1.0
    along = np.einsum("qbr,ql->rbl", mix, axial)
    norms = np.zeros(COEFS)
    for i in range(CUBE):
        plane = np.einsum("rbl,bj->rjl", along, planar[:, i])
        norms += np.sum(np.where(ball[i], plane, 0.0) ** 2, axis=(1, 2))
    mix /= np.sqrt(norms)
    return planar, axial, mix


def plane_pairs(slab):
    planar, _, _ = tables()
    count = planar.shape[0]
    starts = range(-slab, CUBE + slab)
    out = np.zeros((2 * count, len(starts), LANES), ml_dtypes.bfloat16)
    high, low = halves(planar)
    for at, a in enumerate(starts):
        for side in range(2):
            if 0 <= a + side < CUBE:
                lanes = slice(side * CUBE, (side + 1) * CUBE)
                out[:count, at, lanes] = high[:, a + side]
                out[count:, at, lanes] = low[:, a + side]
    return out.reshape(2 * count, len(starts) * LANES)


def axial_windows(nz):
    _, axial, _ = tables()
    high, low = halves(axial)
    out = np.zeros((nz // CUBE, 2 * DEGREES, 2 * LANES), ml_dtypes.bfloat16)
    for tile in range(nz // CUBE):
        offset = tile * CUBE - window_start(tile * CUBE, nz)
        out[tile, :DEGREES, offset : offset + CUBE] = high
        out[tile, DEGREES:, offset : offset + CUBE] = low
    return out


def window_start(z, nz):
    if isinstance(z, int):
        return min(z // LANES * LANES, nz - 2 * LANES)
    return jnp.minimum(lax.shift_right_logical(z, 7) * LANES, nz - 2 * LANES)


def mix_table():
    _, _, mix = tables()
    count = mix.shape[1]
    high, low = halves(mix)
    out = np.zeros((DEGREES, 2 * count, COEFS), ml_dtypes.bfloat16)
    out[:, :count], out[:, count:] = high, low
    return out


def dot(a, b):
    return jnp.dot(a, b, preferred_element_type=F32)


def split(value):
    high = value.astype(BF16)
    return high, (value - high.astype(F32)).astype(BF16)


def iota(shape, axis):
    return lax.broadcasted_iota(jnp.int32, shape, axis)


def lookup(index, scalars, first):
    out = jnp.zeros(index.shape, F32)
    for at in range(scalars.shape[0]):
        out = jnp.where(index == at + first, scalars[at], out)
    return out


def columns(row):
    eye = iota((GROUP, GROUP), 0) == iota((GROUP, GROUP), 1)
    ones = jnp.ones((GROUP, GROUP), BF16)
    spread = jnp.where(eye, row, 0.0)
    out, rest = None, spread
    for _ in range(3):
        part = rest.astype(BF16)
        rest = rest - part.astype(F32)
        term = dot(part, ones)
        out = term if out is None else out + term
    return out


def columns_small(row):
    eye = iota((GROUP, GROUP), 0) == iota((GROUP, GROUP), 1)
    return dot(jnp.where(eye, row, 0.0).astype(BF16), jnp.ones((GROUP, GROUP), BF16))


def stencil(field, previous, speed, kinds, states, pole_ref, loss_ref, out, shift):
    slab, rows, nz = previous.shape
    groups, chunks = nz // LANES, rows // 8
    lane, sub = iota((8, LANES), 1), iota((8, LANES), 0)
    first_lane, last_lane = lane == 0, lane == LANES - 1
    first_sub, last_sub = sub == 0, sub == 7
    pole = jnp.zeros((8, LANES), F32)
    gain = jnp.zeros((8, LANES), F32)
    for at in range(pole_ref.shape[0]):
        pole = jnp.where(lane == at + 1, pole_ref[at], pole)
        gain = jnp.where(lane == at + 1, loss_ref[at] * (1.0 - pole_ref[at]), gain)

    def tile(ref, x, j, g):
        return ref[x, 8 * j : 8 * j + 8, LANES * g : LANES * (g + 1)]

    def body(x, carry):
        centre = {}
        for j in range(chunks):
            for g in range(groups):
                centre[j, g] = tile(field, x + 1, j, g)
        for j in range(chunks):
            for g in range(groups):
                here = centre[j, g]
                left = pltpu.roll(here, 1, 1)
                left = jnp.where(
                    first_lane, pltpu.roll(centre[j, g - 1], 1, 1) if g else 0.0, left
                )
                right = pltpu.roll(here, LANES - 1, 1)
                right = jnp.where(
                    last_lane,
                    pltpu.roll(centre[j, g + 1], LANES - 1, 1) if g + 1 < groups else 0.0,
                    right,
                )
                up = pltpu.roll(here, 1, 0)
                up = jnp.where(first_sub, pltpu.roll(centre[j - 1, g], 1, 0) if j else 0.0, up)
                down = pltpu.roll(here, 7, 0)
                down = jnp.where(
                    last_sub, pltpu.roll(centre[j + 1, g], 7, 0) if j + 1 < chunks else 0.0, down
                )
                beside = tile(field, x, j, g) + tile(field, x + 2, j, g)
                beside = beside + up + down + left + right
                value = 2.0 * here - tile(previous, x, j, g)
                value = value + tile(speed, x, j, g).astype(F32) * (beside - 6.0 * here)
                at = pl.ds((x * rows + 8 * j) * groups + g, 8, stride=groups)
                kind = kinds[at, :].astype(jnp.int32)
                state = jnp.take_along_axis(pole, kind, axis=1) * states[at, :]
                state = state + jnp.take_along_axis(gain, kind, axis=1) * value
                states[at, :] = state
                out[x + shift, 8 * j : 8 * j + 8, LANES * g : LANES * (g + 1)] = value - state
        return carry

    lax.fori_loop(0, slab, body, 0)


def first_step(
    cell_ref, pole_ref, loss_ref, now, prev, speed, cells, material, state,
    out, kinds, states, field, lanes, kind_cols, state_cols,
):
    slab, rows, nz = prev.shape
    nodes = cells.shape[1]
    field[0] = jnp.zeros((rows, nz), F32)
    field[slab + 1] = jnp.zeros((rows, nz), F32)
    for x in range(slab):
        field[x + 1] = now[x]
    kinds[...] = jnp.zeros_like(kinds)
    states[...] = jnp.zeros_like(states)
    scaled = lookup(material[...], loss_ref, 0) * state[...]
    kind_row = (material[...] + 1).astype(F32)
    lane_row = (cells[...] & (LANES - 1)).astype(F32)
    for at in range(nodes // GROUP):
        part = slice(at * GROUP, (at + 1) * GROUP)
        lanes[part, :] = columns_small(lane_row[:, part])
        kind_cols[part, :] = columns_small(kind_row[:, part])
        state_cols[part, :] = columns(scaled[:, part])
    lane = iota((1, LANES), 1).astype(F32)

    def place(k, carry):
        row = pl.ds(lax.shift_right_logical(cell_ref[0, k], 7), 1)
        source = pl.ds(k, 1)
        mask = lanes[source, :] == lane
        pltpu.store(kinds.at[row, :], kind_cols[source, :], mask=mask)
        pltpu.store(states.at[row, :], state_cols[source, :], mask=mask)
        return carry

    lax.fori_loop(0, nodes, place, 0, unroll=8)
    stencil(field, prev, speed, kinds, states, pole_ref, loss_ref, out, 0)


def add_rows(value, speed, low, high):
    rows = value.shape[0]
    row = iota(value.shape, 0)
    term = jnp.where(row == 0, low, jnp.where(row == rows - 1, high, 0.0))
    return value + speed * term


def send_planes(first, last, top, bottom, c_first, c_last, c_top, c_bottom,
                x_low, x_high, y_low, y_high, sx_low, sx_high, sy_low, sy_high):
    slab = top.shape[0]
    for at, value, speed, halo, out in (
        (0, first, c_first, x_low, sx_low),
        (slab - 1, last, c_last, x_high, sx_high),
    ):
        c = speed[0].astype(F32)
        plane = value[0] + c * halo[...].astype(F32)
        low = y_low[at : at + 1, :].astype(F32)
        high = y_high[at : at + 1, :].astype(F32)
        out[...] = add_rows(plane, c, low, high).astype(BF16)
    for value, speed, halo, out, r, xr in (
        (top, c_top, y_low, sy_low, 0, 0),
        (bottom, c_bottom, y_high, sy_high, top.shape[1] - 1, x_low.shape[0] - 1),
    ):
        rows = []
        for x in range(slab):
            c = speed[x, r : r + 1, :].astype(F32)
            line = value[x, r : r + 1, :] + c * halo[x : x + 1, :].astype(F32)
            if x == 0:
                line = line + c * x_low[xr : xr + 1, :].astype(F32)
            if x == slab - 1:
                line = line + c * x_high[xr : xr + 1, :].astype(F32)
            rows.append(line)
        out[...] = jnp.concatenate(rows, axis=0).astype(BF16)


def fix_halo(field, speed, x_low, x_high, y_low, y_high, shift):
    slab, rows, _ = speed.shape
    for x in range(slab):
        at = x + shift
        if x == 0:
            field[at] = field[at] + speed[x].astype(F32) * x_low[...].astype(F32)
        if x == slab - 1:
            field[at] = field[at] + speed[x].astype(F32) * x_high[...].astype(F32)
        c = speed[x, 0:1, :].astype(F32)
        field[at, 0:1, :] = field[at, 0:1, :] + c * y_low[x : x + 1, :].astype(F32)
        c = speed[x, rows - 1 : rows, :].astype(F32)
        last = slice(rows - 1, rows)
        field[at, last, :] = field[at, last, :] + c * y_high[x : x + 1, :].astype(F32)


def second_step(
    cell_ref, pole_ref, loss_ref, now, prev, speed, kinds, states_in, cells, material,
    x_low, x_high, y_low, y_high, before, out, filter_out, field, states, picked,
):
    slab, rows, nz = prev.shape
    nodes = cells.shape[1]
    field[0] = jnp.zeros((rows, nz), F32)
    field[slab + 1] = jnp.zeros((rows, nz), F32)
    for x in range(slab):
        field[x + 1] = now[x]
    states[...] = states_in[...]
    fix_halo(field, speed, x_low, x_high, y_low, y_high, 1)
    for x in range(slab):
        before[x] = field[x + 1]
    stencil(field, prev, speed, kinds, states, pole_ref, loss_ref, out, 0)

    def pick(k, carry):
        row = lax.shift_right_logical(cell_ref[0, k], 7)
        picked[pl.ds(k, 1), :] = states[pl.ds(row, 1), :]
        return carry

    lax.fori_loop(0, nodes, pick, 0, unroll=8)
    lane_row = (cells[...] & (LANES - 1)).astype(F32)
    inverse = 1.0 / lookup(material[...], loss_ref, 0)
    lane = iota((GROUP, LANES), 1).astype(F32)
    for at in range(nodes // GROUP):
        part = slice(at * GROUP, (at + 1) * GROUP)
        chosen = jnp.where(columns_small(lane_row[:, part]) == lane, picked[part, :], 0.0)
        line = lax.dot_general(
            jnp.ones((8, LANES), F32), chosen, (((1,), (1,)), ((), ())),
            precision=lax.Precision.HIGHEST, preferred_element_type=F32,
        )
        filter_out[:, part] = line[0:1, :] * inverse[:, part]


def fit(anchor_ref, place_ref, pressure_in, speed, x_low, x_high, y_low, y_high,
        pairs, axial, mix, pressure, partial, *products):
    slab, rows, nz = speed.shape
    spheres = partial.shape[0]
    count = pairs.shape[0] // 2
    x_first, y_first, s_first = place_ref[0], place_ref[1], place_ref[2]
    for x in range(slab):
        pressure[x] = pressure_in[x]
    fix_halo(pressure, speed, x_low, x_high, y_low, y_high, 0)
    limit = CUBE * CUBE
    odd_y = 2 * iota((CUBE, 2 * LANES), 0) - (CUBE - 1)
    y_square = odd_y * odd_y
    lane = iota((CUBE, 2 * LANES), 1)
    products[1][...] = jnp.zeros_like(products[1])

    def sphere(s, carry):
        base = 3 * (s_first + s)
        x0 = anchor_ref[base]
        y0 = pl.multiple_of(anchor_ref[base + 1] - y_first, CUBE)
        z0 = anchor_ref[base + 2]
        start = pl.multiple_of(window_start(z0, nz), LANES)
        odd_z = 2 * (lane - (z0 - start)) - (CUBE - 1)
        square = y_square + odd_z * odd_z
        a0 = x_first - x0
        planes = []
        for i in range(slab):
            odd_x = 2 * (a0 + i) - (CUBE - 1)
            cells = pressure[i, pl.ds(y0, CUBE), pl.ds(start, 2 * LANES)]
            planes.append(jnp.where(square <= limit - odd_x * odd_x, cells, 0.0).astype(BF16))
        blank = jnp.zeros((LANES - 2 * CUBE, 2 * LANES), BF16)
        total = None
        first = jnp.clip(a0, -slab, CUBE) + slab
        left, right = [], []
        for i in range(0, slab, 2):
            at = pl.multiple_of(jnp.minimum(first + i, CUBE + 2 * slab - 1) * LANES, LANES)
            left.append(pairs[:, pl.ds(at, LANES)])
            right += [planes[i], planes[i + 1], blank]
        total = dot(jnp.concatenate(left, axis=1), jnp.concatenate(right, axis=0))
        high, low = split(total[:count] + total[count:])
        tile = lax.shift_right_logical(z0 * 1366, 16)
        factor = axial[tile]
        contract = (((1,), (1,)), ((), ()))
        one = lax.dot_general(factor, high, contract, preferred_element_type=F32)
        two = lax.dot_general(factor[:DEGREES], low, contract, preferred_element_type=F32)
        moment = one[:DEGREES] + one[DEGREES:] + two
        at = pl.ds(pl.multiple_of(s * DEGREES, DEGREES), DEGREES)
        products[0][at, :] = moment[:, :LANES]
        products[1][at, 0 : count - LANES] = moment[:, LANES:]
        return carry

    lax.fori_loop(0, spheres, sphere, 0, unroll=2)
    result = jnp.zeros((spheres, COEFS), F32)
    for q in range(DEGREES):
        at = pl.ds(q, spheres, stride=DEGREES)
        moment = jnp.concatenate([products[0][at, :], products[1][at, :]], axis=1)
        high, low = split(moment[:, :count])
        upper, lower = mix[q, :count], mix[q, count:]
        result = result + (dot(high, upper) + (dot(low, upper) + dot(high, lower)))
    partial[...] = result


def whole(memory=pltpu.VMEM):
    return pl.BlockSpec(memory_space=memory)


def shards(now, prev, speed, node_cell, node_material, filter_state, pole, loss, anchors):
    slab, rows, nz = now.shape
    nodes = node_cell.shape[-1]
    slabs, parts = lax.axis_size("gx"), lax.axis_size("gy")
    gx, gy = lax.axis_index("gx"), lax.axis_index("gy")
    spheres = anchors.shape[0] // parts
    cells = node_cell.reshape(1, nodes)
    material = node_material.reshape(1, nodes)
    state = filter_state.reshape(1, nodes)
    dense = jax.ShapeDtypeStruct((slab * rows * nz // LANES, LANES), F32)
    block = jax.ShapeDtypeStruct((slab, rows, nz), F32)
    params = pltpu.CompilerParams(vmem_limit_bytes=56 << 20)

    def up(count):
        return [(i, i + 1) for i in range(count - 1)]

    def down(count):
        return [(i + 1, i) for i in range(count - 1)]

    def exchange(x_first, x_last, y_first, y_last):
        return (
            lax.ppermute(x_last, "gx", up(slabs)),
            lax.ppermute(x_first, "gx", down(slabs)),
            lax.ppermute(y_last, "gy", up(parts)),
            lax.ppermute(y_first, "gy", down(parts)),
        )

    halo = exchange(
        now[0].astype(BF16), now[-1].astype(BF16),
        now[:, 0, :].astype(BF16), now[:, -1, :].astype(BF16),
    )
    half, kinds, states = pl.pallas_call(
        first_step,
        out_shape=(block, dense, dense),
        in_specs=[whole(pltpu.SMEM)] * 3 + [whole()] * 6,
        out_specs=(whole(),) * 3,
        scratch_shapes=[pltpu.VMEM((slab + 2, rows, nz), F32)]
        + [pltpu.VMEM((nodes, LANES), F32)] * 3,
        compiler_params=params,
        name="first_step",
    )(cells, pole, loss, now, prev, speed, cells, material, state)

    def plane_at(x):
        return pl.BlockSpec((1, rows, nz), lambda i: (x, 0, 0))

    def rows_at(y, height):
        return pl.BlockSpec((slab, height, nz), lambda i: (0, y // height, 0))

    edges = [plane_at(0), plane_at(slab - 1), rows_at(0, 16), rows_at(rows - 16, 16)]
    sent = pl.pallas_call(
        send_planes,
        grid=(1,),
        out_shape=(jax.ShapeDtypeStruct((rows, nz), BF16),) * 2
        + (jax.ShapeDtypeStruct((slab, nz), BF16),) * 2,
        in_specs=edges + edges + [whole()] * 4,
        out_specs=(whole(),) * 4,
        compiler_params=params,
        name="send_planes",
    )(half, half, half, half, speed, speed, speed, speed, *halo)
    halo_next = exchange(*sent)
    before, partly, filter_out = pl.pallas_call(
        second_step,
        out_shape=(block, block, jax.ShapeDtypeStruct((1, nodes), F32)),
        in_specs=[whole(pltpu.SMEM)] * 3 + [whole()] * 11,
        out_specs=(whole(),) * 3,
        scratch_shapes=[
            pltpu.VMEM((slab + 2, rows, nz), F32),
            pltpu.VMEM(dense.shape, F32),
            pltpu.VMEM((nodes, LANES), F32),
        ],
        compiler_params=params,
        name="second_step",
    )(cells, pole, loss, half, now, speed, kinds, states, cells, material, *halo)
    place = jnp.stack([gx * slab, gy * rows, gy * spheres]).astype(jnp.int32)
    pressure, partial = pl.pallas_call(
        fit,
        out_shape=(block, jax.ShapeDtypeStruct((spheres, COEFS), F32)),
        in_specs=[whole(pltpu.SMEM)] * 2 + [whole()] * 9,
        out_specs=(whole(),) * 2,
        scratch_shapes=[pltpu.VMEM((spheres * DEGREES, LANES), F32)] * 2,
        compiler_params=params,
        name="fit",
    )(
        anchors.reshape(-1), place, partly, speed, *halo_next,
        jnp.asarray(plane_pairs(slab)), jnp.asarray(axial_windows(nz)), jnp.asarray(mix_table()),
    )
    coefficients = jnp.sum(lax.all_gather(partial, "gx", axis=0, tiled=False), axis=0)
    return pressure, before, filter_out.reshape(filter_state.shape), coefficients


def solution(mesh):
    grid = P("gx", "gy", None)
    return jax.shard_map(
        shards,
        mesh=mesh,
        in_specs=(grid,) * 6 + (P(), P(), P()),
        out_specs=(grid, grid, grid, P("gy", None)),
        check_vma=False,
    )
```

```python
import functools
import math

import jax
import jax.numpy as jnp
import ml_dtypes
import numpy as np
from jax import lax
from jax.experimental import pallas as pl
from jax.experimental.pallas import tpu as pltpu
from jax.sharding import PartitionSpec as P

CUBE = 48
COEFS = 256
DEGREES = 16
LANES = 128
GROUP = 128
F32 = jnp.float32
BF16 = jnp.bfloat16


def halves(table):
    high = table.astype(ml_dtypes.bfloat16)
    low = (table - high.astype(np.float64)).astype(ml_dtypes.bfloat16)
    return high, low


@functools.lru_cache(maxsize=None)
def tables():
    axis = (np.arange(CUBE) + 0.5 - CUBE / 2.0) / (CUBE / 2.0)
    u, v = np.meshgrid(axis, axis, indexing="ij")
    planar_index, planar = {}, []
    for degree in range(DEGREES):
        for m in range(degree % 2, degree + 1, 2):
            k = (degree - m) // 2
            value = (-(u + 1j * v)) ** m * (u * u + v * v) ** k
            for part in range(2 if m else 1):
                planar_index[m, k, part] = len(planar)
                planar.append(value.imag if part else value.real)
    planar = np.stack(planar)
    axial = np.stack([axis**q for q in range(DEGREES)])
    poly = {}
    for m in range(DEGREES):
        poly[m, m] = {0: 1.0}
        for n in range(m + 1, DEGREES):
            entry = {}
            for k, c in poly[n - 1, m].items():
                entry[k] = entry.get(k, 0.0) + (2 * n - 1) * c
            for k, c in poly.get((n - 2, m), {}).items():
                entry[k] = entry.get(k, 0.0) - c
                entry[k + 1] = entry.get(k + 1, 0.0) - c
            poly[n, m] = {k: c / ((n - m) * (n + m)) for k, c in entry.items()}
    mix = np.zeros((DEGREES, len(planar), COEFS))
    row = 0
    for n in range(DEGREES):
        for m in range(n + 1):
            for part in range(2 if m else 1):
                for k, c in poly[n, m].items():
                    mix[n - m - 2 * k, planar_index[m, k, part], row] = c
                row += 1
    ball = (
        axis[:, None, None] ** 2 + axis[None, :, None] ** 2 + axis[None, None, :] ** 2
    ) <= 1.0
    along = np.einsum("qbr,ql->rbl", mix, axial)
    norms = np.zeros(COEFS)
    for i in range(CUBE):
        plane = np.einsum("rbl,bj->rjl", along, planar[:, i])
        norms += np.sum(np.where(ball[i], plane, 0.0) ** 2, axis=(1, 2))
    mix /= np.sqrt(norms)
    return planar, axial, mix


def plane_pairs(slab):
    planar, _, _ = tables()
    count = planar.shape[0]
    starts = range(-slab, CUBE + slab)
    out = np.zeros((2 * count, len(starts), LANES), ml_dtypes.bfloat16)
    high, low = halves(planar)
    for at, a in enumerate(starts):
        for side in range(2):
            if 0 <= a + side < CUBE:
                lanes = slice(side * CUBE, (side + 1) * CUBE)
                out[:count, at, lanes] = high[:, a + side]
                out[count:, at, lanes] = low[:, a + side]
    return out.reshape(2 * count, len(starts) * LANES)


def axial_windows(nz):
    _, axial, _ = tables()
    high, low = halves(axial)
    out = np.zeros((nz // CUBE, 2 * DEGREES, 2 * LANES), ml_dtypes.bfloat16)
    for tile in range(nz // CUBE):
        offset = tile * CUBE - window_start(tile * CUBE, nz)
        out[tile, :DEGREES, offset : offset + CUBE] = high
        out[tile, DEGREES:, offset : offset + CUBE] = low
    return out


def window_start(z, nz):
    if isinstance(z, int):
        return min(z // LANES * LANES, nz - 2 * LANES)
    return jnp.minimum(lax.shift_right_logical(z, 7) * LANES, nz - 2 * LANES)


def mix_rows(q):
    sizes = [-(-(DEGREES - at) * (DEGREES + 1 - at) // 2 // 16) * 16 for at in range(DEGREES)]
    return sum(sizes[:q]), sizes[q]


def mix_table():
    _, _, mix = tables()
    high, low = halves(mix)
    first, size = mix_rows(DEGREES - 1)
    out = np.zeros((2, first + size, COEFS), ml_dtypes.bfloat16)
    for q in range(DEGREES):
        first, size = mix_rows(q)
        size = min(size, mix.shape[1])
        out[0, first : first + size] = high[q, :size]
        out[1, first : first + size] = low[q, :size]
    return out


def dot(a, b):
    return jnp.dot(a, b, preferred_element_type=F32)


def split(value):
    high = value.astype(BF16)
    return high, (value - high.astype(F32)).astype(BF16)


def iota(shape, axis):
    return lax.broadcasted_iota(jnp.int32, shape, axis)


def lookup(index, scalars, first):
    out = jnp.zeros(index.shape, F32)
    for at in range(scalars.shape[0]):
        out = jnp.where(index == at + first, scalars[at], out)
    return out


def columns(row):
    eye = iota((GROUP, GROUP), 0) == iota((GROUP, GROUP), 1)
    ones = jnp.ones((GROUP, GROUP), BF16)
    spread = jnp.where(eye, row, 0.0)
    out, rest = None, spread
    for _ in range(3):
        part = rest.astype(BF16)
        rest = rest - part.astype(F32)
        term = dot(part, ones)
        out = term if out is None else out + term
    return out


def columns_small(row):
    eye = iota((GROUP, GROUP), 0) == iota((GROUP, GROUP), 1)
    return dot(jnp.where(eye, row, 0.0).astype(BF16), jnp.ones((GROUP, GROUP), BF16))


def node_maps(
    cell_ref, loss_ref, cells, material, state, kinds, states, lanes, kind_cols, state_cols
):
    nodes = cells.shape[1]
    scaled = lookup(material[...], loss_ref, 0) * state[...]
    kind_row = (material[...] + 1).astype(F32)
    lane_row = (cells[...] & (LANES - 1)).astype(F32)
    for at in range(nodes // GROUP):
        part = slice(at * GROUP, (at + 1) * GROUP)
        lanes[part, :] = columns_small(lane_row[:, part])
        kind_cols[part, :] = columns_small(kind_row[:, part])
        state_cols[part, :] = columns(scaled[:, part])
    kinds[...] = jnp.zeros_like(kinds)
    states[...] = jnp.zeros_like(states)
    lane = iota((1, LANES), 1).astype(F32)

    def place(k, carry):
        row = pl.ds(lax.shift_right_logical(cell_ref[0, k], 7), 1)
        source = pl.ds(k, 1)
        mask = lanes[source, :] == lane
        pltpu.store(kinds.at[row, :], kind_cols[source, :], mask=mask)
        pltpu.store(states.at[row, :], state_cols[source, :], mask=mask)
        return carry

    lax.fori_loop(0, nodes, place, 0, unroll=32)


def stencil(pole_ref, loss_ref, below, here_ref, above, previous, speed, kinds, states, out,
            states_out):
    _, rows, nz = previous.shape
    groups, chunks = nz // LANES, rows // 8
    x, last = pl.program_id(0), pl.num_programs(0) - 1
    lane, sub = iota((8, LANES), 1), iota((8, LANES), 0)
    first_lane, last_lane = lane == 0, lane == LANES - 1
    first_sub, last_sub = sub == 0, sub == 7
    pole = jnp.zeros((8, LANES), F32)
    gain = jnp.zeros((8, LANES), F32)
    for at in range(pole_ref.shape[0]):
        pole = jnp.where(lane == at + 1, pole_ref[at], pole)
        gain = jnp.where(lane == at + 1, loss_ref[at] * (1.0 - pole_ref[at]), gain)
    has_below = jnp.where(x > 0, 1.0, 0.0)
    has_above = jnp.where(x < last, 1.0, 0.0)

    def tile(ref, j, g):
        return ref[0, 8 * j : 8 * j + 8, LANES * g : LANES * (g + 1)]

    for j in range(chunks):
        for g in range(groups):
            here = tile(here_ref, j, g)
            left = pltpu.roll(here, 1, 1)
            left = jnp.where(
                first_lane, pltpu.roll(tile(here_ref, j, g - 1), 1, 1) if g else 0.0, left
            )
            right = pltpu.roll(here, LANES - 1, 1)
            right = jnp.where(
                last_lane,
                pltpu.roll(tile(here_ref, j, g + 1), LANES - 1, 1) if g + 1 < groups else 0.0,
                right,
            )
            up = pltpu.roll(here, 1, 0)
            up = jnp.where(first_sub, pltpu.roll(tile(here_ref, j - 1, g), 1, 0) if j else 0.0, up)
            down = pltpu.roll(here, 7, 0)
            down = jnp.where(
                last_sub,
                pltpu.roll(tile(here_ref, j + 1, g), 7, 0) if j + 1 < chunks else 0.0,
                down,
            )
            beside = has_below * tile(below, j, g) + has_above * tile(above, j, g)
            beside = beside + up + down + left + right
            value = 2.0 * here - tile(previous, j, g)
            value = value + tile(speed, j, g).astype(F32) * (beside - 6.0 * here)
            at = pl.ds(8 * j * groups + g, 8, stride=groups)
            kind = kinds[at, :].astype(jnp.int32)
            state = jnp.take_along_axis(pole, kind, axis=1) * states[at, :]
            state = state + jnp.take_along_axis(gain, kind, axis=1) * value
            states_out[at, :] = state
            out[0, 8 * j : 8 * j + 8, LANES * g : LANES * (g + 1)] = value - state


def flags():
    out = []
    for axis in ("gx", "gy"):
        at = lax.axis_index(axis)
        out.append(jnp.where(at > 0, 1.0, 0.0))
        out.append(jnp.where(at < lax.axis_size(axis) - 1, 1.0, 0.0))
    return out


def edges(first, last, top, bottom, sx_low, sx_high, sy_low, sy_high):
    sx_low[...] = first[0].astype(BF16)
    sx_high[...] = last[0].astype(BF16)
    for x in range(top.shape[0]):
        sy_low[x : x + 1, :] = top[x, 0:1, :].astype(BF16)
        sy_high[x : x + 1, :] = bottom[x, bottom.shape[1] - 1 :, :].astype(BF16)


def fix_planes(first, last, top, bottom, c_first, c_last, c_top, c_bottom, halo):
    x_low, x_high, y_low, y_high = halo
    has = flags()
    slab, rows = top.shape[0], first.shape[1]
    final = top.shape[1] - 1
    for at, value, speed, ref, flag in (
        (0, first, c_first, x_low, has[0]),
        (slab - 1, last, c_last, x_high, has[1]),
    ):
        value[0] = value[0] + speed[0].astype(F32) * (flag * ref[...].astype(F32))
        for row, beside, there in ((0, y_low, has[2]), (rows - 1, y_high, has[3])):
            one = slice(row, row + 1)
            term = speed[0, one, :].astype(F32) * (there * beside[at : at + 1, :].astype(F32))
            value[0, one, :] = value[0, one, :] + term
    for x in range(slab):
        if x in (0, slab - 1):
            plane = first if x == 0 else last
            top[x] = plane[0, : final + 1, :]
            bottom[x] = plane[0, rows - final - 1 :, :]
            continue
        c = c_top[x, 0:1, :].astype(F32)
        top[x, 0:1, :] = top[x, 0:1, :] + c * (has[2] * y_low[x : x + 1, :].astype(F32))
        c = c_bottom[x, 15:16, :].astype(F32)
        term = c * (has[3] * y_high[x : x + 1, :].astype(F32))
        bottom[x, final : final + 1, :] = bottom[x, final : final + 1, :] + term


def fix_and_send(field_in, c_first, c_last, c_top, c_bottom, x_low, x_high, y_low, y_high,
                 field, sx_low, sx_high, sy_low, sy_high, first, last, top, bottom, sems):
    slab, rows = top.shape[0], first.shape[1]
    places = (
        (pl.ds(0, 1), pl.ds(0, rows), first),
        (pl.ds(slab - 1, 1), pl.ds(0, rows), last),
        (pl.ds(0, slab), pl.ds(0, 8), top),
        (pl.ds(0, slab), pl.ds(rows - 8, 8), bottom),
    )
    copies = [
        pltpu.make_async_copy(field_in.at[x, y], ref, sems.at[at])
        for at, (x, y, ref) in enumerate(places)
    ]
    for copy in copies:
        copy.start()
    for copy in copies:
        copy.wait()
    fix_planes(first, last, top, bottom, c_first, c_last, c_top, c_bottom,
               (x_low, x_high, y_low, y_high))
    copies = [
        pltpu.make_async_copy(ref, field.at[x, y], sems.at[at])
        for at, (x, y, ref) in enumerate(places[:2])
    ]
    inner = pl.ds(1, slab - 2)
    copies += [
        pltpu.make_async_copy(ref.at[inner], field.at[inner, y], sems.at[at + 2])
        for at, (_, y, ref) in enumerate(places[2:])
    ]
    for copy in copies:
        copy.start()
    edges(first, last, top, bottom, sx_low, sx_high, sy_low, sy_high)
    for copy in copies:
        copy.wait()


def gather_nodes(cell_ref, loss_ref, states, cells, material, filter_out, picked):
    nodes = cells.shape[1]

    def pick(k, carry):
        row = lax.shift_right_logical(cell_ref[0, k], 7)
        picked[pl.ds(k, 1), :] = states[pl.ds(row, 1), :]
        return carry

    lax.fori_loop(0, nodes, pick, 0, unroll=32)
    lane_row = (cells[...] & (LANES - 1)).astype(F32)
    inverse = 1.0 / lookup(material[...], loss_ref, 0)
    lane = iota((GROUP, LANES), 1).astype(F32)
    for at in range(nodes // GROUP):
        part = slice(at * GROUP, (at + 1) * GROUP)
        chosen = jnp.where(columns_small(lane_row[:, part]) == lane, picked[part, :], 0.0)
        line = lax.dot_general(
            jnp.ones((8, LANES), F32), chosen, (((1,), (1,)), ((), ())),
            precision=lax.Precision.HIGHEST, preferred_element_type=F32,
        )
        filter_out[:, part] = line[0:1, :] * inverse[:, part]


def fit(anchor_ref, pressure_in, c_first, c_last, c_top, c_bottom, x_low, x_high, y_low, y_high,
        pairs, axial, mix, pressure, partial, *products):
    slab, rows, nz = pressure.shape
    spheres = partial.shape[0]
    count = pairs.shape[0] // 2
    x_first = lax.axis_index("gx") * slab
    y_first = lax.axis_index("gy") * rows
    s_first = lax.axis_index("gy") * spheres
    for x in range(slab):
        pressure[x] = pressure_in[x]
    has = flags()
    for at, speed, ref, flag in ((0, c_first, x_low, has[0]), (slab - 1, c_last, x_high, has[1])):
        term = speed[0].astype(F32) * (flag * ref[...].astype(F32))
        pressure[at] = pressure[at] + term
    for x in range(slab):
        for row, speed, r, ref, flag in (
            (0, c_top, 0, y_low, has[2]),
            (rows - 1, c_bottom, 15, y_high, has[3]),
        ):
            one = slice(row, row + 1)
            term = speed[x, r : r + 1, :].astype(F32) * (flag * ref[x : x + 1, :].astype(F32))
            pressure[x, one, :] = pressure[x, one, :] + term
    limit = CUBE * CUBE
    odd_y = 2 * iota((CUBE, 2 * LANES), 0) - (CUBE - 1)
    y_square = odd_y * odd_y
    lane = iota((CUBE, 2 * LANES), 1)
    products[1][...] = jnp.zeros_like(products[1])

    def sphere(s, carry):
        base = s_first + s
        x0 = anchor_ref[base, 0]
        y0 = pl.multiple_of(anchor_ref[base, 1] - y_first, CUBE)
        z0 = anchor_ref[base, 2]
        start = pl.multiple_of(window_start(z0, nz), LANES)
        odd_z = 2 * (lane - (z0 - start)) - (CUBE - 1)
        square = y_square + odd_z * odd_z
        a0 = x_first - x0
        planes = []
        for i in range(slab):
            odd_x = 2 * (a0 + i) - (CUBE - 1)
            cells = pressure[i, pl.ds(y0, CUBE), pl.ds(start, 2 * LANES)]
            planes.append(jnp.where(square <= limit - odd_x * odd_x, cells, 0.0).astype(BF16))
        blank = jnp.zeros((LANES - 2 * CUBE, 2 * LANES), BF16)
        total = None
        first = jnp.clip(a0, -slab, CUBE) + slab
        left, right = [], []
        for i in range(0, slab, 2):
            at = pl.multiple_of(jnp.minimum(first + i, CUBE + 2 * slab - 1) * LANES, LANES)
            left.append(pairs[:, pl.ds(at, LANES)])
            right += [planes[i], planes[i + 1], blank]
        total = dot(jnp.concatenate(left, axis=1), jnp.concatenate(right, axis=0))
        high, low = split(total[:count] + total[count:])
        tile = lax.shift_right_logical(z0 * 1366, 16)
        factor = axial[tile]
        contract = (((1,), (1,)), ((), ()))
        one = lax.dot_general(factor, high, contract, preferred_element_type=F32)
        two = lax.dot_general(factor[:DEGREES], low, contract, preferred_element_type=F32)
        moment = one[:DEGREES] + one[DEGREES:] + two
        at = pl.ds(pl.multiple_of(s * DEGREES, DEGREES), DEGREES)
        products[0][at, :] = moment[:, :LANES]
        products[1][at, 0 : count - LANES] = moment[:, LANES:]
        return carry

    lax.fori_loop(0, spheres, sphere, 0, unroll=4)
    result = jnp.zeros((spheres, COEFS), F32)
    for q in range(DEGREES):
        at = pl.ds(q, spheres, stride=DEGREES)
        moment = jnp.concatenate([products[0][at, :], products[1][at, :]], axis=1)
        first, size = mix_rows(q)
        high, low = split(moment[:, :size])
        upper, lower = mix[0, first : first + size], mix[1, first : first + size]
        result = result + (dot(high, upper) + (dot(low, upper) + dot(high, lower)))
    partial[...] = result


def whole(memory=pltpu.VMEM):
    return pl.BlockSpec(memory_space=memory)


def after(value, *others):
    return lax.optimization_barrier((value, *others))


def shards(now, prev, speed, node_cell, node_material, filter_state, pole, loss, anchors):
    slab, rows, nz = now.shape
    nodes = node_cell.shape[-1]
    spheres = anchors.shape[0] // lax.axis_size("gy")
    per_plane = rows * nz // LANES
    cells = node_cell.reshape(1, nodes)
    material = node_material.reshape(1, nodes)
    state = filter_state.reshape(1, nodes)
    dense = jax.ShapeDtypeStruct((slab * per_plane, LANES), F32)
    block = jax.ShapeDtypeStruct((slab, rows, nz), F32)
    sends = (jax.ShapeDtypeStruct((rows, nz), BF16),) * 2
    sends += (jax.ShapeDtypeStruct((slab, nz), BF16),) * 2
    smem = whole(pltpu.SMEM)

    def params(mebibytes):
        return pltpu.CompilerParams(vmem_limit_bytes=mebibytes << 20)

    def shift(value, axis, step):
        count = lax.axis_size(axis)
        return lax.ppermute(value, axis, [(i, (i + step) % count) for i in range(count)])

    def plane_at(x):
        return pl.BlockSpec((1, rows, nz), lambda i: (x, 0, 0))

    def rows_at(y, height):
        return pl.BlockSpec((slab, height, nz), lambda i: (0, y // height, 0))

    speeds = [speed] * 4
    edge_specs = [plane_at(0), plane_at(slab - 1), rows_at(0, 16), rows_at(rows - 16, 16)]

    def step(centre, previous, kinds, states):
        def plane(move):
            return pl.BlockSpec(
                (1, rows, nz), lambda i: (jnp.clip(i + move, 0, slab - 1), 0, 0)
            )

        map_spec = pl.BlockSpec((per_plane, LANES), lambda i: (i, 0))
        return pl.pallas_call(
            stencil,
            grid=(slab,),
            out_shape=(block, dense),
            in_specs=[smem] * 2 + [plane(-1), plane(0), plane(1), plane(0), plane(0)]
            + [map_spec] * 2,
            out_specs=(plane(0), map_spec),
            compiler_params=params(16),
            name="stencil",
        )(pole, loss, centre, centre, centre, previous, speed, kinds, states)

    x_first, x_last, y_first, y_last = pl.pallas_call(
        edges,
        grid=(1,),
        out_shape=sends,
        in_specs=[plane_at(0), plane_at(slab - 1), rows_at(0, 8), rows_at(rows - 8, 8)],
        out_specs=(whole(),) * 4,
        compiler_params=params(16),
        name="edges",
    )(now, now, now, now)
    x_low = shift(x_last, "gx", 1)
    x_high = shift(x_first, "gx", -1)
    kinds, states = pl.pallas_call(
        node_maps,
        out_shape=(dense, dense),
        in_specs=[smem] * 2 + [whole()] * 3,
        out_specs=(whole(),) * 2,
        scratch_shapes=[pltpu.VMEM((nodes, LANES), F32)] * 3,
        compiler_params=params(16),
        name="node_maps",
    )(cells, loss, cells, material, state)
    y_first, y_last, kinds = after(y_first, y_last, kinds)
    y_low = shift(y_last, "gy", 1)
    y_high = shift(y_first, "gy", -1)
    half, states = step(now, prev, kinds, states)
    before, x_first, x_last, y_first, y_last = pl.pallas_call(
        fix_and_send,
        grid=(1,),
        out_shape=(block,) + sends,
        in_specs=[whole(pl.ANY)] + edge_specs + [whole()] * 4,
        out_specs=(whole(pl.ANY),) + (whole(),) * 4,
        scratch_shapes=[pltpu.VMEM((1, rows, nz), F32)] * 2
        + [pltpu.VMEM((slab, 8, nz), F32)] * 2
        + [pltpu.SemaphoreType.DMA((4,))],
        input_output_aliases={0: 0},
        compiler_params=params(16),
        name="fix_and_send",
    )(half, *speeds, x_low, x_high, y_low, y_high)
    x_low = shift(x_last, "gx", 1)
    x_high = shift(x_first, "gx", -1)
    partly, states = step(before, now, kinds, states)
    y_first, y_last, states = after(y_first, y_last, states)
    y_low = shift(y_last, "gy", 1)
    y_high = shift(y_first, "gy", -1)
    filter_out = pl.pallas_call(
        gather_nodes,
        out_shape=jax.ShapeDtypeStruct((1, nodes), F32),
        in_specs=[smem] * 2 + [whole()] * 3,
        out_specs=whole(),
        scratch_shapes=[pltpu.VMEM((nodes, LANES), F32)],
        compiler_params=params(16),
        name="gather_nodes",
    )(cells, loss, states, cells, material)
    pressure, partial = pl.pallas_call(
        fit,
        grid=(1,),
        out_shape=(block, jax.ShapeDtypeStruct((spheres, COEFS), F32)),
        in_specs=[smem, whole()] + edge_specs + [whole()] * 7,
        out_specs=(whole(),) * 2,
        scratch_shapes=[pltpu.VMEM((spheres * DEGREES, LANES), F32)] * 2,
        compiler_params=params(32),
        name="fit",
    )(
        anchors, partly, *speeds, x_low, x_high, y_low, y_high,
        jnp.asarray(plane_pairs(slab)), jnp.asarray(axial_windows(nz)), jnp.asarray(mix_table()),
    )
    coefficients = jnp.sum(lax.all_gather(partial, "gx", axis=0, tiled=False), axis=0)
    return pressure, before, filter_out.reshape(filter_state.shape), coefficients


def solution(mesh):
    grid = P("gx", "gy", None)
    return jax.shard_map(
        shards,
        mesh=mesh,
        in_specs=(grid,) * 6 + (P(), P(), P()),
        out_specs=(grid, grid, grid, P("gy", None)),
        check_vma=False,
    )
```

```python
import functools
import math

import jax
import jax.numpy as jnp
import ml_dtypes
import numpy as np
from jax import lax
from jax.experimental import pallas as pl
from jax.experimental.pallas import tpu as pltpu
from jax.sharding import PartitionSpec as P

CUBE = 48
COEFS = 256
DEGREES = 16
LANES = 128
GROUP = 128
F32 = jnp.float32
BF16 = jnp.bfloat16


def halves(table):
    high = table.astype(ml_dtypes.bfloat16)
    low = (table - high.astype(np.float64)).astype(ml_dtypes.bfloat16)
    return high, low


@functools.lru_cache(maxsize=None)
def tables():
    axis = (np.arange(CUBE) + 0.5 - CUBE / 2.0) / (CUBE / 2.0)
    u, v = np.meshgrid(axis, axis, indexing="ij")
    planar_index, planar = {}, []
    for degree in range(DEGREES):
        for m in range(degree % 2, degree + 1, 2):
            k = (degree - m) // 2
            value = (-(u + 1j * v)) ** m * (u * u + v * v) ** k
            for part in range(2 if m else 1):
                planar_index[m, k, part] = len(planar)
                planar.append(value.imag if part else value.real)
    planar = np.stack(planar)
    axial = np.stack([axis**q for q in range(DEGREES)])
    poly = {}
    for m in range(DEGREES):
        poly[m, m] = {0: 1.0}
        for n in range(m + 1, DEGREES):
            entry = {}
            for k, c in poly[n - 1, m].items():
                entry[k] = entry.get(k, 0.0) + (2 * n - 1) * c
            for k, c in poly.get((n - 2, m), {}).items():
                entry[k] = entry.get(k, 0.0) - c
                entry[k + 1] = entry.get(k + 1, 0.0) - c
            poly[n, m] = {k: c / ((n - m) * (n + m)) for k, c in entry.items()}
    mix = np.zeros((DEGREES, len(planar), COEFS))
    row = 0
    for n in range(DEGREES):
        for m in range(n + 1):
            for part in range(2 if m else 1):
                for k, c in poly[n, m].items():
                    mix[n - m - 2 * k, planar_index[m, k, part], row] = c
                row += 1
    ball = (
        axis[:, None, None] ** 2 + axis[None, :, None] ** 2 + axis[None, None, :] ** 2
    ) <= 1.0
    along = np.einsum("qbr,ql->rbl", mix, axial)
    norms = np.zeros(COEFS)
    for i in range(CUBE):
        plane = np.einsum("rbl,bj->rjl", along, planar[:, i])
        norms += np.sum(np.where(ball[i], plane, 0.0) ** 2, axis=(1, 2))
    mix /= np.sqrt(norms)
    return planar, axial, mix


def plane_pairs(slab):
    planar, _, _ = tables()
    count = planar.shape[0]
    starts = range(-slab, CUBE + slab)
    out = np.zeros((2 * count, len(starts), LANES), ml_dtypes.bfloat16)
    high, low = halves(planar)
    for at, a in enumerate(starts):
        for side in range(2):
            if 0 <= a + side < CUBE:
                lanes = slice(side * CUBE, (side + 1) * CUBE)
                out[:count, at, lanes] = high[:, a + side]
                out[count:, at, lanes] = low[:, a + side]
    return out.reshape(2 * count, len(starts) * LANES)


def axial_windows(nz):
    _, axial, _ = tables()
    high, low = halves(axial)
    out = np.zeros((nz // CUBE, 2 * DEGREES, 2 * LANES), ml_dtypes.bfloat16)
    for tile in range(nz // CUBE):
        offset = tile * CUBE - window_start(tile * CUBE, nz)
        out[tile, :DEGREES, offset : offset + CUBE] = high
        out[tile, DEGREES:, offset : offset + CUBE] = low
    return out


def window_start(z, nz):
    if isinstance(z, int):
        return min(z // LANES * LANES, nz - 2 * LANES)
    return jnp.minimum(lax.shift_right_logical(z, 7) * LANES, nz - 2 * LANES)


def mix_rows(q):
    sizes = [-(-(DEGREES - at) * (DEGREES + 1 - at) // 2 // 16) * 16 for at in range(DEGREES)]
    return sum(sizes[:q]), sizes[q]


def mix_table():
    _, _, mix = tables()
    high, low = halves(mix)
    first, size = mix_rows(DEGREES - 1)
    out = np.zeros((2, first + size, COEFS), ml_dtypes.bfloat16)
    for q in range(DEGREES):
        first, size = mix_rows(q)
        size = min(size, mix.shape[1])
        out[0, first : first + size] = high[q, :size]
        out[1, first : first + size] = low[q, :size]
    return out


def dot(a, b):
    return jnp.dot(a, b, preferred_element_type=F32)


def split(value):
    high = value.astype(BF16)
    return high, (value - high.astype(F32)).astype(BF16)


def iota(shape, axis):
    return lax.broadcasted_iota(jnp.int32, shape, axis)


def lookup(index, scalars, first):
    out = jnp.zeros(index.shape, F32)
    for at in range(scalars.shape[0]):
        out = jnp.where(index == at + first, scalars[at], out)
    return out


def columns(row):
    eye = iota((GROUP, GROUP), 0) == iota((GROUP, GROUP), 1)
    ones = jnp.ones((GROUP, GROUP), BF16)
    spread = jnp.where(eye, row, 0.0)
    out, rest = None, spread
    for _ in range(3):
        part = rest.astype(BF16)
        rest = rest - part.astype(F32)
        term = dot(part, ones)
        out = term if out is None else out + term
    return out


def columns_small(row):
    eye = iota((GROUP, GROUP), 0) == iota((GROUP, GROUP), 1)
    return dot(jnp.where(eye, row, 0.0).astype(BF16), jnp.ones((GROUP, GROUP), BF16))


def node_maps(
    cell_ref, loss_ref, cells, material, state, kinds, states, lanes, kind_cols, state_cols
):
    nodes = cells.shape[1]
    scaled = lookup(material[...], loss_ref, 0) * state[...]
    kind_row = (material[...] + 1).astype(F32)
    lane_row = (cells[...] & (LANES - 1)).astype(F32)
    for at in range(nodes // GROUP):
        part = slice(at * GROUP, (at + 1) * GROUP)
        lanes[part, :] = columns_small(lane_row[:, part])
        kind_cols[part, :] = columns_small(kind_row[:, part])
        state_cols[part, :] = columns(scaled[:, part])
    kinds[...] = jnp.zeros_like(kinds)
    states[...] = jnp.zeros_like(states)
    lane = iota((1, LANES), 1).astype(F32)

    def place(k, carry):
        row = pl.ds(lax.shift_right_logical(cell_ref[0, k], 7), 1)
        source = pl.ds(k, 1)
        mask = lanes[source, :] == lane
        pltpu.store(kinds.at[row, :], kind_cols[source, :], mask=mask)
        pltpu.store(states.at[row, :], state_cols[source, :], mask=mask)
        return carry

    lax.fori_loop(0, nodes, place, 0, unroll=32)


def stencil(start, last, pole_ref, loss_ref, below, here_ref, above, previous, speed, kinds,
            states, *outs):
    copies = len(outs) in (3, 6)
    out, states_out = outs[-3:-1] if copies else outs[-2:]
    _, rows, nz = previous.shape
    groups, chunks = nz // LANES, rows // 8
    x = start + pl.program_id(0)
    lane, sub = iota((8, LANES), 1), iota((8, LANES), 0)
    first_lane, last_lane = lane == 0, lane == LANES - 1
    first_sub, last_sub = sub == 0, sub == 7
    pole = jnp.zeros((8, LANES), F32)
    gain = jnp.zeros((8, LANES), F32)
    for at in range(pole_ref.shape[0]):
        pole = jnp.where(lane == at + 1, pole_ref[at], pole)
        gain = jnp.where(lane == at + 1, loss_ref[at] * (1.0 - pole_ref[at]), gain)
    has_below = jnp.where(x > 0, 1.0, 0.0)
    has_above = jnp.where(x < last, 1.0, 0.0)

    def tile(ref, j, g):
        return ref[0, 8 * j : 8 * j + 8, LANES * g : LANES * (g + 1)]

    def row_tiles(j):
        tiles = [tile(here_ref, j, g) for g in range(groups)]
        return tiles, [pltpu.roll(t, 1, 0) for t in tiles], [pltpu.roll(t, 7, 0) for t in tiles]

    zero = jnp.zeros((8, LANES), F32)
    blank = [zero] * groups
    behind, current = (blank,) * 3, row_tiles(0)
    for j in range(chunks):
        ahead = row_tiles(j + 1) if j + 1 < chunks else (blank,) * 3
        heres, downs, ups = current
        lefts = [zero] + [pltpu.roll(t, 1, 1) for t in heres]
        rights = [pltpu.roll(t, LANES - 1, 1) for t in heres] + [zero]
        for g in range(groups):
            here = heres[g]
            left = jnp.where(first_lane, lefts[g], lefts[g + 1])
            right = jnp.where(last_lane, rights[g + 1], rights[g])
            up = jnp.where(first_sub, behind[1][g], downs[g])
            down = jnp.where(last_sub, ahead[2][g], ups[g])
            beside = has_below * tile(below, j, g) + has_above * tile(above, j, g)
            beside = beside + up + down + left + right
            value = 2.0 * here - tile(previous, j, g)
            value = value + tile(speed, j, g).astype(F32) * (beside - 6.0 * here)
            at = pl.ds(8 * j * groups + g, 8, stride=groups)
            kind = kinds[at, :].astype(jnp.int32)
            state = jnp.take_along_axis(pole, kind, axis=1) * states[at, :]
            state = state + jnp.take_along_axis(gain, kind, axis=1) * value
            states_out[at, :] = state
            out[0, 8 * j : 8 * j + 8, LANES * g : LANES * (g + 1)] = value - state
            if copies:
                outs[-1][0, 8 * j : 8 * j + 8, LANES * g : LANES * (g + 1)] = here
        behind, current = current, ahead


def received(one, two, axis):
    at = lax.axis_index(axis)
    even = lax.rem(at, 2) == 0
    one, two = one[...].astype(F32), two[...].astype(F32)
    has_low = jnp.where(at > 0, 1.0, 0.0)
    has_high = jnp.where(at < lax.axis_size(axis) - 1, 1.0, 0.0)
    return has_low * jnp.where(even, two, one), has_high * jnp.where(even, one, two)


def paired(low, high, axis):
    even = lax.rem(lax.axis_index(axis), 2) == 0
    return jnp.where(even, high, low).astype(BF16), jnp.where(even, low, high).astype(BF16)


def edges(first, last, top, bottom, sx_one, sx_two, sy_one, sy_two):
    sx_one[...], sx_two[...] = paired(first[0], last[0], "gx")
    final = bottom.shape[1] - 1
    for x in range(top.shape[0]):
        line = slice(x, x + 1)
        sy_one[line, :], sy_two[line, :] = paired(
            top[x, 0:1, :], bottom[x, final : final + 1, :], "gy"
        )


def edge_places(slab, rows):
    return (
        (pl.ds(0, 1), pl.ds(0, rows)),
        (pl.ds(slab - 1, 1), pl.ds(0, rows)),
        (pl.ds(0, slab), pl.ds(0, 8)),
        (pl.ds(0, slab), pl.ds(rows - 8, 8)),
    )


def first_edges(field, sx_one, sx_two, sy_one, sy_two, first, last, top, bottom, sems):
    layers = (first, last, top, bottom)
    copies = [
        pltpu.make_async_copy(field.at[x, y], ref, sems.at[at])
        for at, ((x, y), ref) in enumerate(zip(edge_places(*field.shape[:2]), layers))
    ]
    for copy in copies:
        copy.start()
    for copy in copies:
        copy.wait()
    edges(*layers, sx_one, sx_two, sy_one, sy_two)


def fix_planes(first, last, top, bottom, c_first, c_last, c_top, c_bottom, x_halo, y_halo):
    slab, rows = top.shape[0], first.shape[1]
    final = top.shape[1] - 1
    for at, value, speed, halo in (
        (0, first, c_first, x_halo[0]),
        (slab - 1, last, c_last, x_halo[1]),
    ):
        value[0] = value[0] + speed[0].astype(F32) * halo
        for row, beside in ((0, y_halo[0]), (rows - 1, y_halo[1])):
            one = slice(row, row + 1)
            term = speed[0, one, :].astype(F32) * beside[at : at + 1, :]
            value[0, one, :] = value[0, one, :] + term
    top[0], bottom[0] = first[0, :8, :], first[0, rows - 8 :, :]
    top[slab - 1], bottom[slab - 1] = last[0, :8, :], last[0, rows - 8 :, :]
    for x in range(1, slab - 1):
        term = c_top[x, 0:1, :].astype(F32) * y_halo[0][x : x + 1, :]
        top[x, 0:1, :] = top[x, 0:1, :] + term
        term = c_bottom[x, 15:16, :].astype(F32) * y_halo[1][x : x + 1, :]
        bottom[x, final : final + 1, :] = bottom[x, final : final + 1, :] + term


def fix_and_send(field_in, c_first, c_last, c_top, c_bottom, x_one, x_two, y_one, y_two,
                 field, sx_one, sx_two, sy_one, sy_two, first, last, top, bottom, sems):
    slab, rows = top.shape[0], first.shape[1]
    places = (
        (pl.ds(0, 1), pl.ds(0, rows), first),
        (pl.ds(slab - 1, 1), pl.ds(0, rows), last),
        (pl.ds(0, slab), pl.ds(0, 8), top),
        (pl.ds(0, slab), pl.ds(rows - 8, 8), bottom),
    )
    copies = [
        pltpu.make_async_copy(field_in.at[x, y], ref, sems.at[at])
        for at, (x, y, ref) in enumerate(places)
    ]
    for copy in copies:
        copy.start()
    for copy in copies:
        copy.wait()
    fix_planes(first, last, top, bottom, c_first, c_last, c_top, c_bottom,
               received(x_one, x_two, "gx"), received(y_one, y_two, "gy"))
    copies = [
        pltpu.make_async_copy(ref, field.at[x, y], sems.at[at])
        for at, (x, y, ref) in enumerate(places[:2])
    ]
    inner = pl.ds(1, slab - 2)
    copies += [
        pltpu.make_async_copy(ref.at[inner], field.at[inner, y], sems.at[at + 2])
        for at, (_, y, ref) in enumerate(places[2:])
    ]
    for copy in copies:
        copy.start()
    edges(first, last, top, bottom, sx_one, sx_two, sy_one, sy_two)
    for copy in copies:
        copy.wait()


def gather_nodes(cell_ref, loss_ref, states, cells, material, filter_out, picked):
    nodes = cells.shape[1]

    def pick(k, carry):
        row = lax.shift_right_logical(cell_ref[0, k], 7)
        picked[pl.ds(k, 1), :] = states[pl.ds(row, 1), :]
        return carry

    lax.fori_loop(0, nodes, pick, 0, unroll=32)
    lane_row = (cells[...] & (LANES - 1)).astype(F32)
    inverse = 1.0 / lookup(material[...], loss_ref, 0)
    lane = iota((GROUP, LANES), 1).astype(F32)
    ones = jnp.ones((8, LANES), BF16)
    for at in range(nodes // GROUP):
        part = slice(at * GROUP, (at + 1) * GROUP)
        rest = jnp.where(columns_small(lane_row[:, part]) == lane, picked[part, :], 0.0)
        line = jnp.zeros((8, GROUP), F32)
        for _ in range(3):
            piece = rest.astype(BF16)
            rest = rest - piece.astype(F32)
            line = line + lax.dot_general(
                ones, piece, (((1,), (1,)), ((), ())), preferred_element_type=F32
            )
        filter_out[:, part] = line[0:1, :] * inverse[:, part]


def finish(cell_ref, loss_ref, anchor_ref, pressure_in, states_in, cells, material,
           c_first, c_last, c_top, c_bottom, x_one, x_two, y_one, y_two,
           pairs_in, axial_in, mix_in, pressure_out, partial, filter_out,
           pressure, states, pairs, axial, mix, picked, planar, products_low, products_high, sems):
    slab, rows, nz = pressure.shape
    spheres = partial.shape[0]
    count = pairs.shape[0] // 2
    incoming = [
        pltpu.make_async_copy(source, target, sems.at[at])
        for at, (source, target) in enumerate((
            (states_in, states), (pressure_in, pressure), (pairs_in, pairs),
            (axial_in, axial), (mix_in, mix),
        ))
    ]
    for copy in incoming:
        copy.start()
    products = (products_low, products_high)
    products_high[...] = jnp.zeros_like(products_high)
    incoming[0].wait()
    gather_nodes(cell_ref, loss_ref, states, cells, material, filter_out, picked)
    incoming[1].wait()
    x_first = lax.axis_index("gx") * slab
    y_first = lax.axis_index("gy") * rows
    s_first = lax.axis_index("gy") * spheres
    x_halo, y_halo = received(x_one, x_two, "gx"), received(y_one, y_two, "gy")
    for at, speed, halo in ((0, c_first, x_halo[0]), (slab - 1, c_last, x_halo[1])):
        pressure[at] = pressure[at] + speed[0].astype(F32) * halo
    for x in range(slab):
        for row, speed, r, halo in ((0, c_top, 0, y_halo[0]), (rows - 1, c_bottom, 15, y_halo[1])):
            one = slice(row, row + 1)
            term = speed[x, r : r + 1, :].astype(F32) * halo[x : x + 1, :]
            pressure[x, one, :] = pressure[x, one, :] + term
    outgoing = pltpu.make_async_copy(pressure, pressure_out, sems.at[0])
    outgoing.start()
    for copy in incoming[2:]:
        copy.wait()
    limit = CUBE * CUBE
    odd_y = 2 * iota((CUBE, 2 * LANES), 0) - (CUBE - 1)
    y_square = odd_y * odd_y
    lane = iota((CUBE, 2 * LANES), 1)

    def across(s, carry):
        x0 = anchor_ref[0, s_first + s]
        y0 = pl.multiple_of(anchor_ref[1, s_first + s] - y_first, CUBE)
        z0 = anchor_ref[2, s_first + s]
        start = pl.multiple_of(window_start(z0, nz), LANES)
        odd_z = 2 * (lane - (z0 - start)) - (CUBE - 1)
        square = y_square + odd_z * odd_z
        a0 = x_first - x0
        planes = []
        for i in range(slab):
            odd_x = 2 * (a0 + i) - (CUBE - 1)
            values = pressure[i, pl.ds(y0, CUBE), pl.ds(start, 2 * LANES)]
            planes.append(jnp.where(square <= limit - odd_x * odd_x, values, 0.0).astype(BF16))
        blank = jnp.zeros((LANES - 2 * CUBE, 2 * LANES), BF16)
        first = jnp.clip(a0, -slab, CUBE) + slab
        left, right = [], []
        for i in range(0, slab, 2):
            at = pl.multiple_of(jnp.minimum(first + i, CUBE + 2 * slab - 1) * LANES, LANES)
            left.append(pairs[:, pl.ds(at, LANES)])
            right += [planes[i], planes[i + 1], blank]
        total = dot(jnp.concatenate(left, axis=1), jnp.concatenate(right, axis=0))
        planar[s] = total[:count] + total[count:]
        return carry

    def along(s, carry):
        high, low = split(planar[s])
        factor = axial[lax.shift_right_logical(anchor_ref[2, s_first + s] * 1366, 16)]
        contract = (((1,), (1,)), ((), ()))
        one = lax.dot_general(factor, high, contract, preferred_element_type=F32)
        two = lax.dot_general(factor[:DEGREES], low, contract, preferred_element_type=F32)
        moment = one[:DEGREES] + one[DEGREES:] + two
        at = pl.ds(pl.multiple_of(s * DEGREES, DEGREES), DEGREES)
        products[0][at, :] = moment[:, :LANES]
        products[1][at, 0 : count - LANES] = moment[:, LANES:]
        return carry

    lax.fori_loop(0, spheres, across, 0, unroll=4)
    lax.fori_loop(0, spheres, along, 0, unroll=8)
    result = jnp.zeros((spheres, COEFS), F32)
    for q in range(DEGREES):
        at = pl.ds(q, spheres, stride=DEGREES)
        moment = jnp.concatenate([products[0][at, :], products[1][at, :]], axis=1)
        first, size = mix_rows(q)
        high, low = split(moment[:, :size])
        upper, lower = mix[0, first : first + size], mix[1, first : first + size]
        result = result + (dot(high, upper) + (dot(low, upper) + dot(high, lower)))
    partial[...] = result
    outgoing.wait()


def whole(memory=pltpu.VMEM):
    return pl.BlockSpec(memory_space=memory)


def after(value, *others):
    return lax.optimization_barrier((value, *others))


def shards(now, prev, speed, node_cell, node_material, filter_state, pole, loss, anchors):
    slab, rows, nz = now.shape
    nodes = node_cell.shape[-1]
    spheres = anchors.shape[0] // lax.axis_size("gy")
    per_plane = rows * nz // LANES
    cells = node_cell.reshape(1, nodes)
    material = node_material.reshape(1, nodes)
    state = filter_state.reshape(1, nodes)
    dense = jax.ShapeDtypeStruct((slab * per_plane, LANES), F32)
    block = jax.ShapeDtypeStruct((slab, rows, nz), F32)
    sends = (jax.ShapeDtypeStruct((rows, nz), BF16),) * 2
    sends += (jax.ShapeDtypeStruct((slab, nz), BF16),) * 2
    smem = whole(pltpu.SMEM)

    def params(mebibytes):
        return pltpu.CompilerParams(vmem_limit_bytes=mebibytes << 20)

    def swap(value, axis, side):
        count = lax.axis_size(axis)
        moves = [1 - 2 * (i % 2) if side == 0 else 2 * (i % 2) - 1 for i in range(count)]
        return lax.ppermute(value, axis, [(i, (i + moves[i]) % count) for i in range(count)])

    def plane_at(x):
        return pl.BlockSpec((1, rows, nz), lambda i: (x, 0, 0))

    def rows_at(y, height):
        return pl.BlockSpec((slab, height, nz), lambda i: (0, y // height, 0))

    speeds = [speed] * 4
    edge_specs = [plane_at(0), plane_at(slab - 1), rows_at(0, 16), rows_at(rows - 16, 16)]

    def step(centre, previous, kinds, states, part, limit, copies, done=()):
        start, stop = part

        def plane(move):
            return pl.BlockSpec(
                (1, rows, nz), lambda i: (jnp.clip(i + start + move, 0, slab - 1), 0, 0)
            )

        map_spec = pl.BlockSpec((per_plane, LANES), lambda i: (i + start, 0))
        return pl.pallas_call(
            functools.partial(stencil, start, slab - 1),
            grid=(stop - start,),
            out_shape=(block, dense) + (block,) * copies,
            in_specs=[smem] * 2 + [plane(-1), plane(0), plane(1), plane(0), plane(0)]
            + [map_spec] * 2 + [whole(pl.ANY)] * len(done),
            out_specs=(plane(0), map_spec) + (plane(0),) * copies,
            input_output_aliases={9 + at: at for at in range(len(done))},
            compiler_params=params(limit),
            name="stencil",
        )(pole, loss, centre, centre, centre, previous, speed, kinds, states, *done)

    layers = [pltpu.VMEM((1, rows, nz), F32)] * 2 + [pltpu.VMEM((slab, 8, nz), F32)] * 2
    layers += [pltpu.SemaphoreType.DMA((4,))]
    sx_one, sx_two, sy_one, sy_two = pl.pallas_call(
        first_edges,
        out_shape=sends,
        in_specs=[whole(pltpu.HBM)],
        out_specs=(whole(),) * 4,
        scratch_shapes=layers,
        compiler_params=params(16),
        name="edges",
    )(now)
    x_one, x_two = swap(sx_one, "gx", 0), swap(sx_two, "gx", 1)
    kinds, states = pl.pallas_call(
        node_maps,
        out_shape=(dense, dense),
        in_specs=[smem] * 2 + [whole()] * 3,
        out_specs=(whole(),) * 2,
        scratch_shapes=[pltpu.VMEM((nodes, LANES), F32)] * 3,
        compiler_params=params(16),
        name="node_maps",
    )(cells, loss, cells, material, state)
    sy_one, sy_two, kinds = after(sy_one, sy_two, kinds)
    y_one, y_two = swap(sy_one, "gy", 0), swap(sy_two, "gy", 1)
    half, states = step(now, prev, kinds, states, (0, slab), 16, False)
    half, sx_one, sx_two, sy_one, sy_two = pl.pallas_call(
        fix_and_send,
        grid=(1,),
        out_shape=(block,) + sends,
        in_specs=[whole(pl.ANY)] + edge_specs + [whole()] * 4,
        out_specs=(whole(pl.ANY),) + (whole(),) * 4,
        scratch_shapes=layers,
        input_output_aliases={0: 0},
        compiler_params=params(16),
        name="fix_and_send",
    )(half, *speeds, x_one, x_two, y_one, y_two)
    x_one, x_two = swap(sx_one, "gx", 0), swap(sx_two, "gx", 1)
    first_part = step(half, now, kinds, states, (0, slab // 2), 16, True)
    sy_one, sy_two, *first_part = after(sy_one, sy_two, *first_part)
    y_one, y_two = swap(sy_one, "gy", 0), swap(sy_two, "gy", 1)
    partly, states, before = step(
        half, now, kinds, states, (slab // 2, slab), 16, True, first_part
    )
    fit_tables = (plane_pairs(slab), axial_windows(nz), mix_table())
    pressure, partial, filter_out = pl.pallas_call(
        finish,
        grid=(1,),
        out_shape=(
            block,
            jax.ShapeDtypeStruct((spheres, COEFS), F32),
            jax.ShapeDtypeStruct((1, nodes), F32),
        ),
        in_specs=[smem] * 3 + [whole(pl.ANY)] * 2 + [whole()] * 2 + edge_specs + [whole()] * 4
        + [whole(pltpu.HBM)] * 3,
        out_specs=(whole(pl.ANY), whole(), whole()),
        scratch_shapes=[pltpu.VMEM(block.shape, F32), pltpu.VMEM(dense.shape, F32)]
        + [pltpu.VMEM(table.shape, BF16) for table in fit_tables]
        + [
            pltpu.VMEM((nodes, LANES), F32),
            pltpu.VMEM((spheres, fit_tables[0].shape[0] // 2, 2 * LANES), F32),
            pltpu.VMEM((spheres * DEGREES, LANES), F32),
            pltpu.VMEM((spheres * DEGREES, LANES), F32),
            pltpu.SemaphoreType.DMA((5,)),
        ],
        compiler_params=params(32),
        name="finish",
    )(
        cells, loss, anchors.T, partly, states, cells, material, *speeds,
        x_one, x_two, y_one, y_two, *(jnp.asarray(table) for table in fit_tables),
    )
    if lax.axis_size("gx") == 8:
        partial = partial + swap(partial, "gx", 0)
        others = [
            lax.ppermute(partial, "gx", [(i, i ^ move) for i in range(8)]) for move in (2, 4, 6)
        ]
        coefficients = (partial + others[0]) + (others[1] + others[2])
    else:
        coefficients = jnp.sum(lax.all_gather(partial, "gx", axis=0, tiled=False), axis=0)
    return pressure, before, filter_out.reshape(filter_state.shape), coefficients


def solution(mesh):
    grid = P("gx", "gy", None)
    return jax.shard_map(
        shards,
        mesh=mesh,
        in_specs=(grid,) * 6 + (P(), P(), P()),
        out_specs=(grid, grid, grid, P("gy", None)),
        check_vma=False,
    )
```

```python
import functools
import math

import jax
import jax.numpy as jnp
import ml_dtypes
import numpy as np
from jax import lax
from jax.experimental import pallas as pl
from jax.experimental.pallas import tpu as pltpu
from jax.sharding import PartitionSpec as P

CUBE = 48
COEFS = 256
DEGREES = 16
LANES = 128
GROUP = 128
F32 = jnp.float32
BF16 = jnp.bfloat16


def halves(table):
    high = table.astype(ml_dtypes.bfloat16)
    low = (table - high.astype(np.float64)).astype(ml_dtypes.bfloat16)
    return high, low


@functools.lru_cache(maxsize=None)
def tables():
    axis = (np.arange(CUBE) + 0.5 - CUBE / 2.0) / (CUBE / 2.0)
    u, v = np.meshgrid(axis, axis, indexing="ij")
    planar_index, planar = {}, []
    for degree in range(DEGREES):
        for m in range(degree % 2, degree + 1, 2):
            k = (degree - m) // 2
            value = (-(u + 1j * v)) ** m * (u * u + v * v) ** k
            for part in range(2 if m else 1):
                planar_index[m, k, part] = len(planar)
                planar.append(value.imag if part else value.real)
    planar = np.stack(planar)
    axial = np.stack([axis**q for q in range(DEGREES)])
    poly = {}
    for m in range(DEGREES):
        poly[m, m] = {0: 1.0}
        for n in range(m + 1, DEGREES):
            entry = {}
            for k, c in poly[n - 1, m].items():
                entry[k] = entry.get(k, 0.0) + (2 * n - 1) * c
            for k, c in poly.get((n - 2, m), {}).items():
                entry[k] = entry.get(k, 0.0) - c
                entry[k + 1] = entry.get(k + 1, 0.0) - c
            poly[n, m] = {k: c / ((n - m) * (n + m)) for k, c in entry.items()}
    mix = np.zeros((DEGREES, len(planar), COEFS))
    row = 0
    for n in range(DEGREES):
        for m in range(n + 1):
            for part in range(2 if m else 1):
                for k, c in poly[n, m].items():
                    mix[n - m - 2 * k, planar_index[m, k, part], row] = c
                row += 1
    ball = (
        axis[:, None, None] ** 2 + axis[None, :, None] ** 2 + axis[None, None, :] ** 2
    ) <= 1.0
    along = np.einsum("qbr,ql->rbl", mix, axial)
    norms = np.zeros(COEFS)
    for i in range(CUBE):
        plane = np.einsum("rbl,bj->rjl", along, planar[:, i])
        norms += np.sum(np.where(ball[i], plane, 0.0) ** 2, axis=(1, 2))
    mix /= np.sqrt(norms)
    return planar, axial, mix


def plane_pairs(slab):
    planar, _, _ = tables()
    count = planar.shape[0]
    starts = range(-slab, CUBE + slab)
    out = np.zeros((2 * count, len(starts), LANES), ml_dtypes.bfloat16)
    high, low = halves(planar)
    for at, a in enumerate(starts):
        for side in range(2):
            if 0 <= a + side < CUBE:
                lanes = slice(side * CUBE, (side + 1) * CUBE)
                out[:count, at, lanes] = high[:, a + side]
                out[count:, at, lanes] = low[:, a + side]
    return out.reshape(2 * count, len(starts) * LANES)


def axial_windows(nz):
    _, axial, _ = tables()
    high, low = halves(axial)
    out = np.zeros((nz // CUBE, 2 * DEGREES, 2 * LANES), ml_dtypes.bfloat16)
    for tile in range(nz // CUBE):
        offset = tile * CUBE - window_start(tile * CUBE, nz)
        out[tile, :DEGREES, offset : offset + CUBE] = high
        out[tile, DEGREES:, offset : offset + CUBE] = low
    return out


def window_start(z, nz):
    if isinstance(z, int):
        return min(z // LANES * LANES, nz - 2 * LANES)
    return jnp.minimum(lax.shift_right_logical(z, 7) * LANES, nz - 2 * LANES)


def mix_rows(q):
    sizes = [-(-(DEGREES - at) * (DEGREES + 1 - at) // 2 // 16) * 16 for at in range(DEGREES)]
    return sum(sizes[:q]), sizes[q]


def mix_table():
    _, _, mix = tables()
    high, low = halves(mix)
    first, size = mix_rows(DEGREES - 1)
    out = np.zeros((2, first + size, COEFS), ml_dtypes.bfloat16)
    for q in range(DEGREES):
        first, size = mix_rows(q)
        size = min(size, mix.shape[1])
        out[0, first : first + size] = high[q, :size]
        out[1, first : first + size] = low[q, :size]
    return out


def dot(a, b):
    return jnp.dot(a, b, preferred_element_type=F32)


def split(value):
    high = value.astype(BF16)
    return high, (value - high.astype(F32)).astype(BF16)


def iota(shape, axis):
    return lax.broadcasted_iota(jnp.int32, shape, axis)


def lookup(index, scalars, first):
    out = jnp.zeros(index.shape, F32)
    for at in range(scalars.shape[0]):
        out = jnp.where(index == at + first, scalars[at], out)
    return out


def columns(row):
    eye = iota((GROUP, GROUP), 0) == iota((GROUP, GROUP), 1)
    ones = jnp.ones((GROUP, GROUP), BF16)
    spread = jnp.where(eye, row, 0.0)
    out, rest = None, spread
    for _ in range(3):
        part = rest.astype(BF16)
        rest = rest - part.astype(F32)
        term = dot(part, ones)
        out = term if out is None else out + term
    return out


def columns_small(row):
    eye = iota((GROUP, GROUP), 0) == iota((GROUP, GROUP), 1)
    return dot(jnp.where(eye, row, 0.0).astype(BF16), jnp.ones((GROUP, GROUP), BF16))


def node_maps(
    cell_ref, loss_ref, cells, material, state, kinds, states, lanes, kind_cols, state_cols
):
    nodes = cells.shape[1]
    scaled = lookup(material[...], loss_ref, 0) * state[...]
    kind_row = (material[...] + 1).astype(F32)
    lane_row = (cells[...] & (LANES - 1)).astype(F32)
    for at in range(nodes // GROUP):
        part = slice(at * GROUP, (at + 1) * GROUP)
        lanes[part, :] = columns_small(lane_row[:, part])
        kind_cols[part, :] = columns_small(kind_row[:, part])
        state_cols[part, :] = columns(scaled[:, part])
    kinds[...] = jnp.zeros_like(kinds)
    states[...] = jnp.zeros_like(states)
    lane = iota((1, LANES), 1).astype(F32)

    def place(k, carry):
        row = pl.ds(lax.shift_right_logical(cell_ref[0, k], 7), 1)
        source = pl.ds(k, 1)
        mask = lanes[source, :] == lane
        pltpu.store(kinds.at[row, :], kind_cols[source, :], mask=mask)
        pltpu.store(states.at[row, :], state_cols[source, :], mask=mask)
        return carry

    lax.fori_loop(0, nodes, place, 0, unroll=32)


def stencil(start, last, pole_ref, loss_ref, below, here_ref, above, previous, speed, kinds,
            states, *outs):
    copies = len(outs) in (3, 6)
    out, states_out = outs[-3:-1] if copies else outs[-2:]
    _, rows, nz = previous.shape
    groups, chunks = nz // LANES, rows // 8
    x = start + pl.program_id(0)
    lane, sub = iota((8, LANES), 1), iota((8, LANES), 0)
    first_lane, last_lane = lane == 0, lane == LANES - 1
    first_sub, last_sub = sub == 0, sub == 7
    pole = jnp.zeros((8, LANES), F32)
    gain = jnp.zeros((8, LANES), F32)
    for at in range(pole_ref.shape[0]):
        pole = jnp.where(lane == at + 1, pole_ref[at], pole)
        gain = jnp.where(lane == at + 1, loss_ref[at] * (1.0 - pole_ref[at]), gain)
    has_below = jnp.where(x > 0, 1.0, 0.0)
    has_above = jnp.where(x < last, 1.0, 0.0)

    def tile(ref, j, g):
        return ref[0, 8 * j : 8 * j + 8, LANES * g : LANES * (g + 1)]

    def row_tiles(j):
        tiles = [tile(here_ref, j, g) for g in range(groups)]
        return tiles, [pltpu.roll(t, 1, 0) for t in tiles], [pltpu.roll(t, 7, 0) for t in tiles]

    zero = jnp.zeros((8, LANES), F32)
    blank = [zero] * groups
    behind, current = (blank,) * 3, row_tiles(0)
    for j in range(chunks):
        ahead = row_tiles(j + 1) if j + 1 < chunks else (blank,) * 3
        heres, downs, ups = current
        lefts = [zero] + [pltpu.roll(t, 1, 1) for t in heres]
        rights = [pltpu.roll(t, LANES - 1, 1) for t in heres] + [zero]
        for g in range(groups):
            here = heres[g]
            left = jnp.where(first_lane, lefts[g], lefts[g + 1])
            right = jnp.where(last_lane, rights[g + 1], rights[g])
            up = jnp.where(first_sub, behind[1][g], downs[g])
            down = jnp.where(last_sub, ahead[2][g], ups[g])
            beside = has_below * tile(below, j, g) + has_above * tile(above, j, g)
            beside = beside + up + down + left + right
            value = 2.0 * here - tile(previous, j, g)
            value = value + tile(speed, j, g).astype(F32) * (beside - 6.0 * here)
            at = pl.ds(8 * j * groups + g, 8, stride=groups)
            kind = kinds[at, :].astype(jnp.int32)
            state = jnp.take_along_axis(pole, kind, axis=1) * states[at, :]
            state = state + jnp.take_along_axis(gain, kind, axis=1) * value
            states_out[at, :] = state
            out[0, 8 * j : 8 * j + 8, LANES * g : LANES * (g + 1)] = value - state
            if copies:
                outs[-1][0, 8 * j : 8 * j + 8, LANES * g : LANES * (g + 1)] = here
        behind, current = current, ahead


def received(one, two, axis):
    at = lax.axis_index(axis)
    even = lax.rem(at, 2) == 0
    one, two = one[...].astype(F32), two[...].astype(F32)
    has_low = jnp.where(at > 0, 1.0, 0.0)
    has_high = jnp.where(at < lax.axis_size(axis) - 1, 1.0, 0.0)
    return has_low * jnp.where(even, two, one), has_high * jnp.where(even, one, two)


def paired(low, high, axis):
    even = lax.rem(lax.axis_index(axis), 2) == 0
    return jnp.where(even, high, low).astype(BF16), jnp.where(even, low, high).astype(BF16)


def edges(first, last, top, bottom, sx_one, sx_two, sy_one, sy_two):
    sx_one[...], sx_two[...] = paired(first[0], last[0], "gx")
    final = bottom.shape[1] - 1
    for x in range(top.shape[0]):
        line = slice(x, x + 1)
        sy_one[line, :], sy_two[line, :] = paired(
            top[x, 0:1, :], bottom[x, final : final + 1, :], "gy"
        )


def fix_planes(first, last, top, bottom, c_first, c_last, c_top, c_bottom, x_halo, y_halo):
    slab, rows = top.shape[0], first.shape[1]
    final = top.shape[1] - 1
    for at, value, speed, halo in (
        (0, first, c_first, x_halo[0]),
        (slab - 1, last, c_last, x_halo[1]),
    ):
        value[0] = value[0] + speed[0].astype(F32) * halo
        for row, beside in ((0, y_halo[0]), (rows - 1, y_halo[1])):
            one = slice(row, row + 1)
            term = speed[0, one, :].astype(F32) * beside[at : at + 1, :]
            value[0, one, :] = value[0, one, :] + term
    top[0], bottom[0] = first[0, :8, :], first[0, rows - 8 :, :]
    top[slab - 1], bottom[slab - 1] = last[0, :8, :], last[0, rows - 8 :, :]
    for x in range(1, slab - 1):
        term = c_top[x, 0:1, :].astype(F32) * y_halo[0][x : x + 1, :]
        top[x, 0:1, :] = top[x, 0:1, :] + term
        term = c_bottom[x, 15:16, :].astype(F32) * y_halo[1][x : x + 1, :]
        bottom[x, final : final + 1, :] = bottom[x, final : final + 1, :] + term


def fix_and_send(field_in, c_first, c_last, c_top, c_bottom, x_one, x_two, y_one, y_two,
                 field, sx_one, sx_two, sy_one, sy_two, first, last, top, bottom, sems):
    slab, rows = top.shape[0], first.shape[1]
    places = (
        (pl.ds(0, 1), pl.ds(0, rows), first),
        (pl.ds(slab - 1, 1), pl.ds(0, rows), last),
        (pl.ds(0, slab), pl.ds(0, 8), top),
        (pl.ds(0, slab), pl.ds(rows - 8, 8), bottom),
    )
    copies = [
        pltpu.make_async_copy(field_in.at[x, y], ref, sems.at[at])
        for at, (x, y, ref) in enumerate(places)
    ]
    for copy in copies:
        copy.start()
    for copy in copies:
        copy.wait()
    fix_planes(first, last, top, bottom, c_first, c_last, c_top, c_bottom,
               received(x_one, x_two, "gx"), received(y_one, y_two, "gy"))
    copies = [
        pltpu.make_async_copy(ref, field.at[x, y], sems.at[at])
        for at, (x, y, ref) in enumerate(places[:2])
    ]
    inner = pl.ds(1, slab - 2)
    copies += [
        pltpu.make_async_copy(ref.at[inner], field.at[inner, y], sems.at[at + 2])
        for at, (_, y, ref) in enumerate(places[2:])
    ]
    for copy in copies:
        copy.start()
    edges(first, last, top, bottom, sx_one, sx_two, sy_one, sy_two)
    for copy in copies:
        copy.wait()


def gather_nodes(cell_ref, loss_ref, states, cells, material, order, filter_out, picked):
    nodes = cells.shape[1]

    def pick(k, carry):
        row = lax.shift_right_logical(cell_ref[0, k], 7)
        picked[pl.ds(k, 1), :] = states[pl.ds(row, 1), :]
        return carry

    lax.fori_loop(0, nodes, pick, 0, unroll=32)
    lane_row = (cells[...] & (LANES - 1)).astype(F32)
    inverse = 1.0 / lookup(material[...], loss_ref, 0)
    lane = iota((GROUP, LANES), 1).astype(F32)
    ones = jnp.ones((8, LANES), BF16)
    for at in range(nodes // GROUP):
        part = slice(at * GROUP, (at + 1) * GROUP)
        rest = jnp.where(columns_small(lane_row[:, part]) == lane, picked[part, :], 0.0)
        line = jnp.zeros((8, GROUP), F32)
        for _ in range(3):
            piece = rest.astype(BF16)
            rest = rest - piece.astype(F32)
            line = line + lax.dot_general(
                ones, piece, (((1,), (1,)), ((), ())), preferred_element_type=F32
            )
        filter_out[:, part] = line[0:1, :] * inverse[:, part]


def finish(anchor_ref, pressure_in, c_first, c_last, c_top, c_bottom, x_one, x_two, y_one, y_two,
           pairs_in, axial_in, mix_in, pressure_out, partial,
           pressure, pairs, axial, mix, planar, products_low, products_high, sems):
    slab, rows, nz = pressure.shape
    spheres = partial.shape[0]
    count = pairs.shape[0] // 2
    incoming = [
        pltpu.make_async_copy(source, target, sems.at[at])
        for at, (source, target) in enumerate((
            (pressure_in, pressure), (pairs_in, pairs), (axial_in, axial), (mix_in, mix),
        ))
    ]
    for copy in incoming:
        copy.start()
    products = (products_low, products_high)
    products_high[...] = jnp.zeros_like(products_high)
    incoming[0].wait()
    x_first = lax.axis_index("gx") * slab
    y_first = lax.axis_index("gy") * rows
    s_first = lax.axis_index("gy") * spheres
    x_halo, y_halo = received(x_one, x_two, "gx"), received(y_one, y_two, "gy")
    for at, speed, halo in ((0, c_first, x_halo[0]), (slab - 1, c_last, x_halo[1])):
        pressure[at] = pressure[at] + speed[0].astype(F32) * halo
    for x in range(slab):
        for row, speed, r, halo in ((0, c_top, 0, y_halo[0]), (rows - 1, c_bottom, 15, y_halo[1])):
            one = slice(row, row + 1)
            term = speed[x, r : r + 1, :].astype(F32) * halo[x : x + 1, :]
            pressure[x, one, :] = pressure[x, one, :] + term
    outgoing = pltpu.make_async_copy(pressure, pressure_out, sems.at[0])
    outgoing.start()
    for copy in incoming[1:]:
        copy.wait()
    limit = CUBE * CUBE
    odd_y = 2 * iota((CUBE, 2 * LANES), 0) - (CUBE - 1)
    y_square = odd_y * odd_y
    lane = iota((CUBE, 2 * LANES), 1)

    def across(s, carry):
        x0 = anchor_ref[0, s_first + s]
        y0 = pl.multiple_of(anchor_ref[1, s_first + s] - y_first, CUBE)
        z0 = anchor_ref[2, s_first + s]
        start = pl.multiple_of(window_start(z0, nz), LANES)
        odd_z = 2 * (lane - (z0 - start)) - (CUBE - 1)
        square = y_square + odd_z * odd_z
        a0 = x_first - x0
        planes = []
        for i in range(slab):
            odd_x = 2 * (a0 + i) - (CUBE - 1)
            values = pressure[i, pl.ds(y0, CUBE), pl.ds(start, 2 * LANES)]
            planes.append(jnp.where(square <= limit - odd_x * odd_x, values, 0.0).astype(BF16))
        blank = jnp.zeros((LANES - 2 * CUBE, 2 * LANES), BF16)
        first = jnp.clip(a0, -slab, CUBE) + slab
        left, right = [], []
        for i in range(0, slab, 2):
            at = pl.multiple_of(jnp.minimum(first + i, CUBE + 2 * slab - 1) * LANES, LANES)
            left.append(pairs[:, pl.ds(at, LANES)])
            right += [planes[i], planes[i + 1], blank]
        total = dot(jnp.concatenate(left, axis=1), jnp.concatenate(right, axis=0))
        planar[s] = total[:count] + total[count:]
        return carry

    def along(s, carry):
        high, low = split(planar[s])
        factor = axial[lax.shift_right_logical(anchor_ref[2, s_first + s] * 1366, 16)]
        contract = (((1,), (1,)), ((), ()))
        one = lax.dot_general(factor, high, contract, preferred_element_type=F32)
        two = lax.dot_general(factor[:DEGREES], low, contract, preferred_element_type=F32)
        moment = one[:DEGREES] + one[DEGREES:] + two
        at = pl.ds(pl.multiple_of(s * DEGREES, DEGREES), DEGREES)
        products[0][at, :] = moment[:, :LANES]
        products[1][at, 0 : count - LANES] = moment[:, LANES:]
        return carry

    lax.fori_loop(0, spheres, across, 0, unroll=8)
    lax.fori_loop(0, spheres, along, 0, unroll=16)
    result = jnp.zeros((spheres, COEFS), F32)
    for q in range(DEGREES):
        at = pl.ds(q, spheres, stride=DEGREES)
        moment = jnp.concatenate([products[0][at, :], products[1][at, :]], axis=1)
        first, size = mix_rows(q)
        high, low = split(moment[:, :size])
        upper, lower = mix[0, first : first + size], mix[1, first : first + size]
        result = result + (dot(high, upper) + (dot(low, upper) + dot(high, lower)))
    partial[...] = result
    outgoing.wait()


def whole(memory=pltpu.VMEM):
    return pl.BlockSpec(memory_space=memory)


def after(value, *others):
    return lax.optimization_barrier((value, *others))


def shards(now, prev, speed, node_cell, node_material, filter_state, pole, loss, anchors):
    slab, rows, nz = now.shape
    nodes = node_cell.shape[-1]
    spheres = anchors.shape[0] // lax.axis_size("gy")
    per_plane = rows * nz // LANES
    cells = node_cell.reshape(1, nodes)
    material = node_material.reshape(1, nodes)
    state = filter_state.reshape(1, nodes)
    dense = jax.ShapeDtypeStruct((slab * per_plane, LANES), F32)
    block = jax.ShapeDtypeStruct((slab, rows, nz), F32)
    sends = (jax.ShapeDtypeStruct((rows, nz), BF16),) * 2
    sends += (jax.ShapeDtypeStruct((slab, nz), BF16),) * 2
    smem = whole(pltpu.SMEM)

    def params(mebibytes):
        return pltpu.CompilerParams(vmem_limit_bytes=mebibytes << 20)

    def swap(value, axis, side):
        count = lax.axis_size(axis)
        moves = [1 - 2 * (i % 2) if side == 0 else 2 * (i % 2) - 1 for i in range(count)]
        return lax.ppermute(value, axis, [(i, (i + moves[i]) % count) for i in range(count)])

    def plane_at(x):
        return pl.BlockSpec((1, rows, nz), lambda i: (x, 0, 0))

    def rows_at(y, height):
        return pl.BlockSpec((slab, height, nz), lambda i: (0, y // height, 0))

    speeds = [speed] * 4
    edge_specs = [plane_at(0), plane_at(slab - 1), rows_at(0, 16), rows_at(rows - 16, 16)]

    def step(centre, previous, kinds, states, part, limit, copies, done=()):
        start, stop = part

        def plane(move):
            return pl.BlockSpec(
                (1, rows, nz), lambda i: (jnp.clip(i + start + move, 0, slab - 1), 0, 0)
            )

        map_spec = pl.BlockSpec((per_plane, LANES), lambda i: (i + start, 0))
        return pl.pallas_call(
            functools.partial(stencil, start, slab - 1),
            grid=(stop - start,),
            out_shape=(block, dense) + (block,) * copies,
            in_specs=[smem] * 2 + [plane(-1), plane(0), plane(1), plane(0), plane(0)]
            + [map_spec] * 2 + [whole(pl.ANY)] * len(done),
            out_specs=(plane(0), map_spec) + (plane(0),) * copies,
            input_output_aliases={9 + at: at for at in range(len(done))},
            compiler_params=params(limit),
            name="stencil",
        )(pole, loss, centre, centre, centre, previous, speed, kinds, states, *done)

    layers = [pltpu.VMEM((1, rows, nz), F32)] * 2 + [pltpu.VMEM((slab, 8, nz), F32)] * 2
    layers += [pltpu.SemaphoreType.DMA((4,))]
    sx_one, sx_two, sy_one, sy_two = pl.pallas_call(
        edges,
        grid=(1,),
        out_shape=sends,
        in_specs=[plane_at(0), plane_at(slab - 1), rows_at(0, 8), rows_at(rows - 8, 8)],
        out_specs=(whole(),) * 4,
        compiler_params=params(16),
        name="edges",
    )(now, now, now, now)
    x_one, x_two = swap(sx_one, "gx", 0), swap(sx_two, "gx", 1)
    y_one, y_two = swap(sy_one, "gy", 0), swap(sy_two, "gy", 1)
    kinds, states = pl.pallas_call(
        node_maps,
        out_shape=(dense, dense),
        in_specs=[smem] * 2 + [whole()] * 3,
        out_specs=(whole(),) * 2,
        scratch_shapes=[pltpu.VMEM((nodes, LANES), F32)] * 3,
        compiler_params=params(16),
        name="node_maps",
    )(cells, loss, cells, material, state)
    (kinds,) = after(kinds)
    half, states = step(now, prev, kinds, states, (0, slab), 16, False)
    half, sx_one, sx_two, sy_one, sy_two = pl.pallas_call(
        fix_and_send,
        grid=(1,),
        out_shape=(block,) + sends,
        in_specs=[whole(pl.ANY)] + edge_specs + [whole()] * 4,
        out_specs=(whole(pl.ANY),) + (whole(),) * 4,
        scratch_shapes=layers,
        input_output_aliases={0: 0},
        compiler_params=params(16),
        name="fix_and_send",
    )(half, *speeds, x_one, x_two, y_one, y_two)
    x_one, x_two = swap(sx_one, "gx", 0), swap(sx_two, "gx", 1)
    first_part = step(half, now, kinds, states, (0, slab // 2), 16, True)
    sy_one, sy_two, *first_part = after(sy_one, sy_two, *first_part)
    y_one, y_two = swap(sy_one, "gy", 0), swap(sy_two, "gy", 1)
    partly, states, before = step(
        half, now, kinds, states, (slab // 2, slab), 16, True, first_part
    )
    fit_tables = (plane_pairs(slab), axial_windows(nz), mix_table())
    pressure, partial = pl.pallas_call(
        finish,
        grid=(1,),
        out_shape=(block, jax.ShapeDtypeStruct((spheres, COEFS), F32)),
        in_specs=[smem, whole(pl.ANY)] + edge_specs + [whole()] * 4 + [whole(pltpu.HBM)] * 3,
        out_specs=(whole(pl.ANY), whole()),
        scratch_shapes=[pltpu.VMEM(block.shape, F32)]
        + [pltpu.VMEM(table.shape, BF16) for table in fit_tables]
        + [
            pltpu.VMEM((spheres, fit_tables[0].shape[0] // 2, 2 * LANES), F32),
            pltpu.VMEM((spheres * DEGREES, LANES), F32),
            pltpu.VMEM((spheres * DEGREES, LANES), F32),
            pltpu.SemaphoreType.DMA((4,)),
        ],
        compiler_params=params(32),
        name="finish",
    )(
        anchors.T, partly, *speeds,
        x_one, x_two, y_one, y_two, *(jnp.asarray(table) for table in fit_tables),
    )
    eight = lax.axis_size("gx") == 8
    if eight:
        partial = partial + swap(partial, "gx", 0)
        others = [
            lax.ppermute(partial, "gx", [(i, i ^ move) for i in range(8)]) for move in (2, 4, 6)
        ]
        coefficients = (partial + others[0]) + (others[1] + others[2])
    else:
        coefficients = jnp.sum(lax.all_gather(partial, "gx", axis=0, tiled=False), axis=0)
    filter_out = pl.pallas_call(
        gather_nodes,
        out_shape=jax.ShapeDtypeStruct((1, nodes), F32),
        in_specs=[smem] * 2 + [whole()] * 3 + [whole(pl.ANY)],
        out_specs=whole(),
        scratch_shapes=[pltpu.VMEM((nodes, LANES), F32)],
        compiler_params=params(16),
        name="gather_nodes",
    )(cells, loss, states, cells, material, partial)
    return pressure, before, filter_out.reshape(filter_state.shape), coefficients


def solution(mesh):
    grid = P("gx", "gy", None)
    return jax.shard_map(
        shards,
        mesh=mesh,
        in_specs=(grid,) * 6 + (P(), P(), P()),
        out_specs=(grid, grid, grid, P("gy", None)),
        check_vma=False,
    )
```

```python
import functools
import math

import jax
import jax.numpy as jnp
import ml_dtypes
import numpy as np
from jax import lax
from jax.experimental import pallas as pl
from jax.experimental.pallas import tpu as pltpu
from jax.sharding import PartitionSpec as P

CUBE = 48
COEFS = 256
DEGREES = 16
LANES = 128
GROUP = 128
F32 = jnp.float32
BF16 = jnp.bfloat16


def halves(table):
    high = table.astype(ml_dtypes.bfloat16)
    low = (table - high.astype(np.float64)).astype(ml_dtypes.bfloat16)
    return high, low


@functools.lru_cache(maxsize=None)
def tables():
    axis = (np.arange(CUBE) + 0.5 - CUBE / 2.0) / (CUBE / 2.0)
    u, v = np.meshgrid(axis, axis, indexing="ij")
    planar_index, planar = {}, []
    for degree in range(DEGREES):
        for m in range(degree % 2, degree + 1, 2):
            k = (degree - m) // 2
            value = (-(u + 1j * v)) ** m * (u * u + v * v) ** k
            for part in range(2 if m else 1):
                planar_index[m, k, part] = len(planar)
                planar.append(value.imag if part else value.real)
    planar = np.stack(planar)
    axial = np.stack([axis**q for q in range(DEGREES)])
    poly = {}
    for m in range(DEGREES):
        poly[m, m] = {0: 1.0}
        for n in range(m + 1, DEGREES):
            entry = {}
            for k, c in poly[n - 1, m].items():
                entry[k] = entry.get(k, 0.0) + (2 * n - 1) * c
            for k, c in poly.get((n - 2, m), {}).items():
                entry[k] = entry.get(k, 0.0) - c
                entry[k + 1] = entry.get(k + 1, 0.0) - c
            poly[n, m] = {k: c / ((n - m) * (n + m)) for k, c in entry.items()}
    mix = np.zeros((DEGREES, len(planar), COEFS))
    row = 0
    for n in range(DEGREES):
        for m in range(n + 1):
            for part in range(2 if m else 1):
                for k, c in poly[n, m].items():
                    mix[n - m - 2 * k, planar_index[m, k, part], row] = c
                row += 1
    ball = (
        axis[:, None, None] ** 2 + axis[None, :, None] ** 2 + axis[None, None, :] ** 2
    ) <= 1.0
    along = np.einsum("qbr,ql->rbl", mix, axial)
    norms = np.zeros(COEFS)
    for i in range(CUBE):
        plane = np.einsum("rbl,bj->rjl", along, planar[:, i])
        norms += np.sum(np.where(ball[i], plane, 0.0) ** 2, axis=(1, 2))
    mix /= np.sqrt(norms)
    return planar, axial, mix


def plane_pairs(slab):
    planar, _, _ = tables()
    count = planar.shape[0]
    starts = range(-slab, CUBE + slab)
    out = np.zeros((2 * count, len(starts), LANES), ml_dtypes.bfloat16)
    high, low = halves(planar)
    for at, a in enumerate(starts):
        for side in range(2):
            if 0 <= a + side < CUBE:
                lanes = slice(side * CUBE, (side + 1) * CUBE)
                out[:count, at, lanes] = high[:, a + side]
                out[count:, at, lanes] = low[:, a + side]
    return out.reshape(2 * count, len(starts) * LANES)


def axial_windows(nz):
    _, axial, _ = tables()
    high, low = halves(axial)
    out = np.zeros((nz // CUBE, 2 * DEGREES, 2 * LANES), ml_dtypes.bfloat16)
    for tile in range(nz // CUBE):
        offset = tile * CUBE - window_start(tile * CUBE, nz)
        out[tile, :DEGREES, offset : offset + CUBE] = high
        out[tile, DEGREES:, offset : offset + CUBE] = low
    return out


def window_start(z, nz):
    if isinstance(z, int):
        return min(z // LANES * LANES, nz - 2 * LANES)
    return jnp.minimum(lax.shift_right_logical(z, 7) * LANES, nz - 2 * LANES)


def mix_rows(q):
    sizes = [-(-(DEGREES - at) * (DEGREES + 1 - at) // 2 // 16) * 16 for at in range(DEGREES)]
    return sum(sizes[:q]), sizes[q]


def mix_table():
    _, _, mix = tables()
    high, low = halves(mix)
    first, size = mix_rows(DEGREES - 1)
    out = np.zeros((2, first + size, COEFS), ml_dtypes.bfloat16)
    for q in range(DEGREES):
        first, size = mix_rows(q)
        size = min(size, mix.shape[1])
        out[0, first : first + size] = high[q, :size]
        out[1, first : first + size] = low[q, :size]
    return out


def dot(a, b):
    return jnp.dot(a, b, preferred_element_type=F32)


def split(value):
    high = value.astype(BF16)
    return high, (value - high.astype(F32)).astype(BF16)


def iota(shape, axis):
    return lax.broadcasted_iota(jnp.int32, shape, axis)


def lookup(index, scalars, first):
    out = jnp.zeros(index.shape, F32)
    for at in range(scalars.shape[0]):
        out = jnp.where(index == at + first, scalars[at], out)
    return out


def columns(row):
    eye = iota((GROUP, GROUP), 0) == iota((GROUP, GROUP), 1)
    ones = jnp.ones((GROUP, GROUP), BF16)
    spread = jnp.where(eye, row, 0.0)
    out, rest = None, spread
    for _ in range(2):
        part = rest.astype(BF16)
        rest = rest - part.astype(F32)
        term = dot(part, ones)
        out = term if out is None else out + term
    return out


def columns_small(row):
    eye = iota((GROUP, GROUP), 0) == iota((GROUP, GROUP), 1)
    return dot(jnp.where(eye, row, 0.0).astype(BF16), jnp.ones((GROUP, GROUP), BF16))


def node_maps(
    cell_ref, loss_ref, cells, material, state, kinds, states, lanes, kind_cols, state_cols
):
    nodes = cells.shape[1]
    scaled = lookup(material[...], loss_ref, 0) * state[...]
    kind_row = (material[...] + 1).astype(F32)
    lane_row = (cells[...] & (LANES - 1)).astype(F32)
    for at in range(nodes // GROUP):
        part = slice(at * GROUP, (at + 1) * GROUP)
        lanes[part, :] = columns_small(lane_row[:, part])
        kind_cols[part, :] = columns_small(kind_row[:, part])
        state_cols[part, :] = columns(scaled[:, part])
    kinds[...] = jnp.zeros_like(kinds)
    states[...] = jnp.zeros_like(states)
    lane = iota((1, LANES), 1).astype(F32)

    def place(k, carry):
        row = pl.ds(lax.shift_right_logical(cell_ref[0, k], 7), 1)
        source = pl.ds(k, 1)
        mask = lanes[source, :] == lane
        pltpu.store(kinds.at[row, :], kind_cols[source, :], mask=mask)
        pltpu.store(states.at[row, :], state_cols[source, :], mask=mask)
        return carry

    lax.fori_loop(0, nodes, place, 0, unroll=32)


def stencil(start, last, pole_ref, loss_ref, below, here_ref, above, previous, speed, kinds,
            states, *outs):
    copies = len(outs) in (3, 6)
    out, states_out = outs[-3:-1] if copies else outs[-2:]
    _, rows, nz = previous.shape
    groups, chunks = nz // LANES, rows // 8
    x = start + pl.program_id(0)
    lane, sub = iota((8, LANES), 1), iota((8, LANES), 0)
    first_lane, last_lane = lane == 0, lane == LANES - 1
    first_sub, last_sub = sub == 0, sub == 7
    pole = jnp.zeros((8, LANES), F32)
    gain = jnp.zeros((8, LANES), F32)
    for at in range(pole_ref.shape[0]):
        pole = jnp.where(lane == at + 1, pole_ref[at], pole)
        gain = jnp.where(lane == at + 1, loss_ref[at] * (1.0 - pole_ref[at]), gain)
    has_below = jnp.where(x > 0, 1.0, 0.0)
    has_above = jnp.where(x < last, 1.0, 0.0)

    def tile(ref, j, g):
        return ref[0, 8 * j : 8 * j + 8, LANES * g : LANES * (g + 1)]

    def row_tiles(j):
        tiles = [tile(here_ref, j, g) for g in range(groups)]
        return tiles, [pltpu.roll(t, 1, 0) for t in tiles], [pltpu.roll(t, 7, 0) for t in tiles]

    zero = jnp.zeros((8, LANES), F32)
    blank = [zero] * groups
    behind, current = (blank,) * 3, row_tiles(0)
    for j in range(chunks):
        ahead = row_tiles(j + 1) if j + 1 < chunks else (blank,) * 3
        heres, downs, ups = current
        lefts = [zero] + [pltpu.roll(t, 1, 1) for t in heres]
        rights = [pltpu.roll(t, LANES - 1, 1) for t in heres] + [zero]
        for g in range(groups):
            here = heres[g]
            left = jnp.where(first_lane, lefts[g], lefts[g + 1])
            right = jnp.where(last_lane, rights[g + 1], rights[g])
            up = jnp.where(first_sub, behind[1][g], downs[g])
            down = jnp.where(last_sub, ahead[2][g], ups[g])
            beside = has_below * tile(below, j, g) + has_above * tile(above, j, g)
            beside = beside + up + down + left + right
            value = 2.0 * here - tile(previous, j, g)
            value = value + tile(speed, j, g).astype(F32) * (beside - 6.0 * here)
            at = pl.ds(8 * j * groups + g, 8, stride=groups)
            kind = kinds[at, :].astype(jnp.int32)
            state = jnp.take_along_axis(pole, kind, axis=1) * states[at, :]
            state = state + jnp.take_along_axis(gain, kind, axis=1) * value
            states_out[at, :] = state
            out[0, 8 * j : 8 * j + 8, LANES * g : LANES * (g + 1)] = value - state
            if copies:
                outs[-1][0, 8 * j : 8 * j + 8, LANES * g : LANES * (g + 1)] = here
        behind, current = current, ahead


def received(one, two, axis):
    at = lax.axis_index(axis)
    even = lax.rem(at, 2) == 0
    one, two = one[...].astype(F32), two[...].astype(F32)
    has_low = jnp.where(at > 0, 1.0, 0.0)
    has_high = jnp.where(at < lax.axis_size(axis) - 1, 1.0, 0.0)
    return has_low * jnp.where(even, two, one), has_high * jnp.where(even, one, two)


def paired(low, high, axis):
    even = lax.rem(lax.axis_index(axis), 2) == 0
    return jnp.where(even, high, low).astype(BF16), jnp.where(even, low, high).astype(BF16)


def edges(first, last, top, bottom, sx_one, sx_two, sy_one, sy_two):
    sx_one[...], sx_two[...] = paired(first[0], last[0], "gx")
    final = bottom.shape[1] - 1
    for x in range(top.shape[0]):
        line = slice(x, x + 1)
        sy_one[line, :], sy_two[line, :] = paired(
            top[x, 0:1, :], bottom[x, final : final + 1, :], "gy"
        )


def fix_planes(first, last, top, bottom, c_first, c_last, c_top, c_bottom, x_halo, y_halo):
    slab, rows = top.shape[0], first.shape[1]
    final = top.shape[1] - 1
    for at, value, speed, halo in (
        (0, first, c_first, x_halo[0]),
        (slab - 1, last, c_last, x_halo[1]),
    ):
        value[0] = value[0] + speed[0].astype(F32) * halo
        for row, beside in ((0, y_halo[0]), (rows - 1, y_halo[1])):
            one = slice(row, row + 1)
            term = speed[0, one, :].astype(F32) * beside[at : at + 1, :]
            value[0, one, :] = value[0, one, :] + term
    top[0], bottom[0] = first[0, :8, :], first[0, rows - 8 :, :]
    top[slab - 1], bottom[slab - 1] = last[0, :8, :], last[0, rows - 8 :, :]
    for x in range(1, slab - 1):
        term = c_top[x, 0:1, :].astype(F32) * y_halo[0][x : x + 1, :]
        top[x, 0:1, :] = top[x, 0:1, :] + term
        term = c_bottom[x, 15:16, :].astype(F32) * y_halo[1][x : x + 1, :]
        bottom[x, final : final + 1, :] = bottom[x, final : final + 1, :] + term


def fix_and_send(field_in, c_first, c_last, c_top, c_bottom, x_one, x_two, y_one, y_two,
                 field, sx_one, sx_two, sy_one, sy_two, first, last, top, bottom, sems):
    slab, rows = top.shape[0], first.shape[1]
    places = (
        (pl.ds(0, 1), pl.ds(0, rows), first),
        (pl.ds(slab - 1, 1), pl.ds(0, rows), last),
        (pl.ds(0, slab), pl.ds(0, 8), top),
        (pl.ds(0, slab), pl.ds(rows - 8, 8), bottom),
    )
    copies = [
        pltpu.make_async_copy(field_in.at[x, y], ref, sems.at[at])
        for at, (x, y, ref) in enumerate(places)
    ]
    for copy in copies:
        copy.start()
    for copy in copies:
        copy.wait()
    fix_planes(first, last, top, bottom, c_first, c_last, c_top, c_bottom,
               received(x_one, x_two, "gx"), received(y_one, y_two, "gy"))
    copies = [
        pltpu.make_async_copy(ref, field.at[x, y], sems.at[at])
        for at, (x, y, ref) in enumerate(places[:2])
    ]
    inner = pl.ds(1, slab - 2)
    copies += [
        pltpu.make_async_copy(ref.at[inner], field.at[inner, y], sems.at[at + 2])
        for at, (_, y, ref) in enumerate(places[2:])
    ]
    for copy in copies:
        copy.start()
    edges(first, last, top, bottom, sx_one, sx_two, sy_one, sy_two)
    for copy in copies:
        copy.wait()


def gather_nodes(cell_ref, loss_ref, states, cells, material, order, filter_out, picked):
    nodes = cells.shape[1]

    def pick(k, carry):
        row = lax.shift_right_logical(cell_ref[0, k], 7)
        picked[pl.ds(k, 1), :] = states[pl.ds(row, 1), :]
        return carry

    lax.fori_loop(0, nodes, pick, 0, unroll=32)
    lane_row = (cells[...] & (LANES - 1)).astype(F32)
    inverse = 1.0 / lookup(material[...], loss_ref, 0)
    lane = iota((GROUP, LANES), 1).astype(F32)
    ones = jnp.ones((8, LANES), BF16)
    for at in range(nodes // GROUP):
        part = slice(at * GROUP, (at + 1) * GROUP)
        rest = jnp.where(columns_small(lane_row[:, part]) == lane, picked[part, :], 0.0)
        line = jnp.zeros((8, GROUP), F32)
        for _ in range(2):
            piece = rest.astype(BF16)
            rest = rest - piece.astype(F32)
            line = line + lax.dot_general(
                ones, piece, (((1,), (1,)), ((), ())), preferred_element_type=F32
            )
        filter_out[:, part] = line[0:1, :] * inverse[:, part]


def finish(anchor_ref, pressure_in, c_first, c_last, c_top, c_bottom, x_one, x_two, y_one, y_two,
           pairs_in, axial_in, mix_in, pressure_out, partial,
           pressure, pairs, axial, mix, planar, products_low, products_high, sems):
    slab, rows, nz = pressure.shape
    spheres = partial.shape[0]
    count = pairs.shape[0] // 2
    incoming = [
        pltpu.make_async_copy(source, target, sems.at[at])
        for at, (source, target) in enumerate((
            (pressure_in, pressure), (pairs_in, pairs), (axial_in, axial), (mix_in, mix),
        ))
    ]
    for copy in incoming:
        copy.start()
    products = (products_low, products_high)
    products_high[...] = jnp.zeros_like(products_high)
    incoming[0].wait()
    x_first = lax.axis_index("gx") * slab
    y_first = lax.axis_index("gy") * rows
    s_first = lax.axis_index("gy") * spheres
    x_halo, y_halo = received(x_one, x_two, "gx"), received(y_one, y_two, "gy")
    for at, speed, halo in ((0, c_first, x_halo[0]), (slab - 1, c_last, x_halo[1])):
        pressure[at] = pressure[at] + speed[0].astype(F32) * halo
    for x in range(slab):
        for row, speed, r, halo in ((0, c_top, 0, y_halo[0]), (rows - 1, c_bottom, 15, y_halo[1])):
            one = slice(row, row + 1)
            term = speed[x, r : r + 1, :].astype(F32) * halo[x : x + 1, :]
            pressure[x, one, :] = pressure[x, one, :] + term
    outgoing = pltpu.make_async_copy(pressure, pressure_out, sems.at[0])
    outgoing.start()
    for copy in incoming[1:]:
        copy.wait()
    limit = CUBE * CUBE
    odd_y = 2 * iota((CUBE, 2 * LANES), 0) - (CUBE - 1)
    y_square = odd_y * odd_y
    lane = iota((CUBE, 2 * LANES), 1)

    def across(s, carry):
        x0 = anchor_ref[0, s_first + s]
        y0 = pl.multiple_of(anchor_ref[1, s_first + s] - y_first, CUBE)
        z0 = anchor_ref[2, s_first + s]
        start = pl.multiple_of(window_start(z0, nz), LANES)
        odd_z = 2 * (lane - (z0 - start)) - (CUBE - 1)
        square = y_square + odd_z * odd_z
        a0 = x_first - x0
        planes = []
        for i in range(slab):
            odd_x = 2 * (a0 + i) - (CUBE - 1)
            values = pressure[i, pl.ds(y0, CUBE), pl.ds(start, 2 * LANES)]
            planes.append(jnp.where(square <= limit - odd_x * odd_x, values, 0.0).astype(BF16))
        blank = jnp.zeros((LANES - 2 * CUBE, 2 * LANES), BF16)
        first = jnp.clip(a0, -slab, CUBE) + slab
        left, right = [], []
        for i in range(0, slab, 2):
            at = pl.multiple_of(jnp.minimum(first + i, CUBE + 2 * slab - 1) * LANES, LANES)
            left.append(pairs[:, pl.ds(at, LANES)])
            right += [planes[i], planes[i + 1], blank]
        total = dot(jnp.concatenate(left, axis=1), jnp.concatenate(right, axis=0))
        planar[s] = total[:count] + total[count:]
        return carry

    def along(s, carry):
        high, low = split(planar[s])
        factor = axial[lax.shift_right_logical(anchor_ref[2, s_first + s] * 1366, 16)]
        contract = (((1,), (1,)), ((), ()))
        one = lax.dot_general(factor, high, contract, preferred_element_type=F32)
        two = lax.dot_general(factor[:DEGREES], low, contract, preferred_element_type=F32)
        moment = one[:DEGREES] + one[DEGREES:] + two
        at = pl.ds(pl.multiple_of(s * DEGREES, DEGREES), DEGREES)
        products[0][at, :] = moment[:, :LANES]
        products[1][at, 0 : count - LANES] = moment[:, LANES:]
        return carry

    lax.fori_loop(0, spheres, across, 0, unroll=8)
    lax.fori_loop(0, spheres, along, 0, unroll=16)
    result = jnp.zeros((spheres, COEFS), F32)
    for q in range(DEGREES):
        at = pl.ds(q, spheres, stride=DEGREES)
        moment = jnp.concatenate([products[0][at, :], products[1][at, :]], axis=1)
        first, size = mix_rows(q)
        high, low = split(moment[:, :size])
        upper, lower = mix[0, first : first + size], mix[1, first : first + size]
        result = result + (dot(high, upper) + (dot(low, upper) + dot(high, lower)))
    partial[...] = result
    outgoing.wait()


def whole(memory=pltpu.VMEM):
    return pl.BlockSpec(memory_space=memory)


def after(value, *others):
    return lax.optimization_barrier((value, *others))


def shards(now, prev, speed, node_cell, node_material, filter_state, pole, loss, anchors):
    slab, rows, nz = now.shape
    nodes = node_cell.shape[-1]
    spheres = anchors.shape[0] // lax.axis_size("gy")
    per_plane = rows * nz // LANES
    cells = node_cell.reshape(1, nodes)
    material = node_material.reshape(1, nodes)
    state = filter_state.reshape(1, nodes)
    dense = jax.ShapeDtypeStruct((slab * per_plane, LANES), F32)
    block = jax.ShapeDtypeStruct((slab, rows, nz), F32)
    sends = (jax.ShapeDtypeStruct((rows, nz), BF16),) * 2
    sends += (jax.ShapeDtypeStruct((slab, nz), BF16),) * 2
    smem = whole(pltpu.SMEM)

    def params(mebibytes):
        return pltpu.CompilerParams(vmem_limit_bytes=mebibytes << 20)

    def swap(value, axis, side):
        count = lax.axis_size(axis)
        moves = [1 - 2 * (i % 2) if side == 0 else 2 * (i % 2) - 1 for i in range(count)]
        return lax.ppermute(value, axis, [(i, (i + moves[i]) % count) for i in range(count)])

    def plane_at(x):
        return pl.BlockSpec((1, rows, nz), lambda i: (x, 0, 0))

    def rows_at(y, height):
        return pl.BlockSpec((slab, height, nz), lambda i: (0, y // height, 0))

    speeds = [speed] * 4
    edge_specs = [plane_at(0), plane_at(slab - 1), rows_at(0, 16), rows_at(rows - 16, 16)]

    def step(centre, previous, kinds, states, part, limit, copies, done=()):
        start, stop = part

        def plane(move):
            return pl.BlockSpec(
                (1, rows, nz), lambda i: (jnp.clip(i + start + move, 0, slab - 1), 0, 0)
            )

        map_spec = pl.BlockSpec((per_plane, LANES), lambda i: (i + start, 0))
        return pl.pallas_call(
            functools.partial(stencil, start, slab - 1),
            grid=(stop - start,),
            out_shape=(block, dense) + (block,) * copies,
            in_specs=[smem] * 2 + [plane(-1), plane(0), plane(1), plane(0), plane(0)]
            + [map_spec] * 2 + [whole(pl.ANY)] * len(done),
            out_specs=(plane(0), map_spec) + (plane(0),) * copies,
            input_output_aliases={9 + at: at for at in range(len(done))},
            compiler_params=params(limit),
            name="stencil",
        )(pole, loss, centre, centre, centre, previous, speed, kinds, states, *done)

    layers = [pltpu.VMEM((1, rows, nz), F32)] * 2 + [pltpu.VMEM((slab, 8, nz), F32)] * 2
    layers += [pltpu.SemaphoreType.DMA((4,))]
    sx_one, sx_two, sy_one, sy_two = pl.pallas_call(
        edges,
        grid=(1,),
        out_shape=sends,
        in_specs=[plane_at(0), plane_at(slab - 1), rows_at(0, 8), rows_at(rows - 8, 8)],
        out_specs=(whole(),) * 4,
        compiler_params=params(16),
        name="edges",
    )(now, now, now, now)
    x_one, x_two = swap(sx_one, "gx", 0), swap(sx_two, "gx", 1)
    y_one, y_two = swap(sy_one, "gy", 0), swap(sy_two, "gy", 1)
    kinds, states = pl.pallas_call(
        node_maps,
        out_shape=(dense, dense),
        in_specs=[smem] * 2 + [whole()] * 3,
        out_specs=(whole(),) * 2,
        scratch_shapes=[pltpu.VMEM((nodes, LANES), F32)] * 3,
        compiler_params=params(16),
        name="node_maps",
    )(cells, loss, cells, material, state)
    (kinds,) = after(kinds)
    half, states = step(now, prev, kinds, states, (0, slab), 16, False)
    half, sx_one, sx_two, sy_one, sy_two = pl.pallas_call(
        fix_and_send,
        grid=(1,),
        out_shape=(block,) + sends,
        in_specs=[whole(pl.ANY)] + edge_specs + [whole()] * 4,
        out_specs=(whole(pl.ANY),) + (whole(),) * 4,
        scratch_shapes=layers,
        input_output_aliases={0: 0},
        compiler_params=params(16),
        name="fix_and_send",
    )(half, *speeds, x_one, x_two, y_one, y_two)
    x_one, x_two = swap(sx_one, "gx", 0), swap(sx_two, "gx", 1)
    first_part = step(half, now, kinds, states, (0, slab // 2), 16, True)
    sy_one, sy_two, *first_part = after(sy_one, sy_two, *first_part)
    y_one, y_two = swap(sy_one, "gy", 0), swap(sy_two, "gy", 1)
    partly, states, before = step(
        half, now, kinds, states, (slab // 2, slab), 16, True, first_part
    )
    fit_tables = (plane_pairs(slab), axial_windows(nz), mix_table())
    pressure, partial = pl.pallas_call(
        finish,
        grid=(1,),
        out_shape=(block, jax.ShapeDtypeStruct((spheres, COEFS), F32)),
        in_specs=[smem, whole(pl.ANY)] + edge_specs + [whole()] * 4 + [whole(pltpu.HBM)] * 3,
        out_specs=(whole(pl.ANY), whole()),
        scratch_shapes=[pltpu.VMEM(block.shape, F32)]
        + [pltpu.VMEM(table.shape, BF16) for table in fit_tables]
        + [
            pltpu.VMEM((spheres, fit_tables[0].shape[0] // 2, 2 * LANES), F32),
            pltpu.VMEM((spheres * DEGREES, LANES), F32),
            pltpu.VMEM((spheres * DEGREES, LANES), F32),
            pltpu.SemaphoreType.DMA((4,)),
        ],
        compiler_params=params(32),
        name="finish",
    )(
        anchors.T, partly, *speeds,
        x_one, x_two, y_one, y_two, *(jnp.asarray(table) for table in fit_tables),
    )
    eight = lax.axis_size("gx") == 8
    if eight:
        partial = partial + swap(partial, "gx", 0)
        others = [
            lax.ppermute(partial, "gx", [(i, i ^ move) for i in range(8)]) for move in (2, 4, 6)
        ]
        coefficients = (partial + others[0]) + (others[1] + others[2])
    else:
        coefficients = jnp.sum(lax.all_gather(partial, "gx", axis=0, tiled=False), axis=0)
    filter_out = pl.pallas_call(
        gather_nodes,
        out_shape=jax.ShapeDtypeStruct((1, nodes), F32),
        in_specs=[smem] * 2 + [whole()] * 3 + [whole(pl.ANY)],
        out_specs=whole(),
        scratch_shapes=[pltpu.VMEM((nodes, LANES), F32)],
        compiler_params=params(16),
        name="gather_nodes",
    )(cells, loss, states, cells, material, partial)
    return pressure, before, filter_out.reshape(filter_state.shape), coefficients


def solution(mesh):
    grid = P("gx", "gy", None)
    return jax.shard_map(
        shards,
        mesh=mesh,
        in_specs=(grid,) * 6 + (P(), P(), P()),
        out_specs=(grid, grid, grid, P("gy", None)),
        check_vma=False,
    )
```

```python
import functools
import math

import jax
import jax.numpy as jnp
import ml_dtypes
import numpy as np
from jax import lax
from jax.experimental import pallas as pl
from jax.experimental.pallas import tpu as pltpu
from jax.sharding import PartitionSpec as P

CUBE = 48
COEFS = 256
DEGREES = 16
LANES = 128
GROUP = 128
F32 = jnp.float32
BF16 = jnp.bfloat16


def halves(table):
    high = table.astype(ml_dtypes.bfloat16)
    low = (table - high.astype(np.float64)).astype(ml_dtypes.bfloat16)
    return high, low


@functools.lru_cache(maxsize=None)
def tables():
    axis = (np.arange(CUBE) + 0.5 - CUBE / 2.0) / (CUBE / 2.0)
    u, v = np.meshgrid(axis, axis, indexing="ij")
    planar_index, planar = {}, []
    for degree in range(DEGREES):
        for m in range(degree % 2, degree + 1, 2):
            k = (degree - m) // 2
            value = (-(u + 1j * v)) ** m * (u * u + v * v) ** k
            for part in range(2 if m else 1):
                planar_index[m, k, part] = len(planar)
                planar.append(value.imag if part else value.real)
    planar = np.stack(planar)
    axial = np.stack([axis**q for q in range(DEGREES)])
    poly = {}
    for m in range(DEGREES):
        poly[m, m] = {0: 1.0}
        for n in range(m + 1, DEGREES):
            entry = {}
            for k, c in poly[n - 1, m].items():
                entry[k] = entry.get(k, 0.0) + (2 * n - 1) * c
            for k, c in poly.get((n - 2, m), {}).items():
                entry[k] = entry.get(k, 0.0) - c
                entry[k + 1] = entry.get(k + 1, 0.0) - c
            poly[n, m] = {k: c / ((n - m) * (n + m)) for k, c in entry.items()}
    mix = np.zeros((DEGREES, len(planar), COEFS))
    row = 0
    for n in range(DEGREES):
        for m in range(n + 1):
            for part in range(2 if m else 1):
                for k, c in poly[n, m].items():
                    mix[n - m - 2 * k, planar_index[m, k, part], row] = c
                row += 1
    ball = (
        axis[:, None, None] ** 2 + axis[None, :, None] ** 2 + axis[None, None, :] ** 2
    ) <= 1.0
    along = np.einsum("qbr,ql->rbl", mix, axial)
    norms = np.zeros(COEFS)
    for i in range(CUBE):
        plane = np.einsum("rbl,bj->rjl", along, planar[:, i])
        norms += np.sum(np.where(ball[i], plane, 0.0) ** 2, axis=(1, 2))
    mix /= np.sqrt(norms)
    return planar, axial, mix


def plane_pairs(slab):
    planar, _, _ = tables()
    count = planar.shape[0]
    starts = range(-slab, CUBE + slab)
    out = np.zeros((2 * count, len(starts), LANES), ml_dtypes.bfloat16)
    high, low = halves(planar)
    for at, a in enumerate(starts):
        for side in range(2):
            if 0 <= a + side < CUBE:
                lanes = slice(side * CUBE, (side + 1) * CUBE)
                out[:count, at, lanes] = high[:, a + side]
                out[count:, at, lanes] = low[:, a + side]
    return out.reshape(2 * count, len(starts) * LANES)


def axial_windows(nz):
    _, axial, _ = tables()
    high, low = halves(axial)
    out = np.zeros((nz // CUBE, 2 * DEGREES, 2 * LANES), ml_dtypes.bfloat16)
    for tile in range(nz // CUBE):
        offset = tile * CUBE - window_start(tile * CUBE, nz)
        out[tile, :DEGREES, offset : offset + CUBE] = high
        out[tile, DEGREES:, offset : offset + CUBE] = low
    return out


def window_start(z, nz):
    if isinstance(z, int):
        return min(z // LANES * LANES, nz - 2 * LANES)
    return jnp.minimum(lax.shift_right_logical(z, 7) * LANES, nz - 2 * LANES)


def mix_rows(q):
    sizes = [-(-(DEGREES - at) * (DEGREES + 1 - at) // 2 // 16) * 16 for at in range(DEGREES)]
    return sum(sizes[:q]), sizes[q]


def mix_table():
    _, _, mix = tables()
    high, low = halves(mix)
    first, size = mix_rows(DEGREES - 1)
    out = np.zeros((2, first + size, COEFS), ml_dtypes.bfloat16)
    for q in range(DEGREES):
        first, size = mix_rows(q)
        size = min(size, mix.shape[1])
        out[0, first : first + size] = high[q, :size]
        out[1, first : first + size] = low[q, :size]
    return out


def dot(a, b):
    return jnp.dot(a, b, preferred_element_type=F32)


def split(value):
    high = value.astype(BF16)
    return high, (value - high.astype(F32)).astype(BF16)


def iota(shape, axis):
    return lax.broadcasted_iota(jnp.int32, shape, axis)


def lookup(index, scalars, first):
    out = jnp.zeros(index.shape, F32)
    for at in range(scalars.shape[0]):
        out = jnp.where(index == at + first, scalars[at], out)
    return out


def columns(row):
    eye = iota((GROUP, GROUP), 0) == iota((GROUP, GROUP), 1)
    ones = jnp.ones((GROUP, GROUP), BF16)
    spread = jnp.where(eye, row, 0.0)
    out, rest = None, spread
    for _ in range(2):
        part = rest.astype(BF16)
        rest = rest - part.astype(F32)
        term = dot(part, ones)
        out = term if out is None else out + term
    return out


def columns_small(row):
    eye = iota((GROUP, GROUP), 0) == iota((GROUP, GROUP), 1)
    return dot(jnp.where(eye, row, 0.0).astype(BF16), jnp.ones((GROUP, GROUP), BF16))


def node_maps(
    cell_ref, loss_ref, cells, material, state, kinds, states, lanes, kind_cols, state_cols
):
    nodes = cells.shape[1]
    scaled = lookup(material[...], loss_ref, 0) * state[...]
    kind_row = (material[...] + 1).astype(F32)
    lane_row = (cells[...] & (LANES - 1)).astype(F32)
    for at in range(nodes // GROUP):
        part = slice(at * GROUP, (at + 1) * GROUP)
        lanes[part, :] = columns_small(lane_row[:, part])
        kind_cols[part, :] = columns_small(kind_row[:, part])
        state_cols[part, :] = columns(scaled[:, part])
    kinds[...] = jnp.zeros_like(kinds)
    states[...] = jnp.zeros_like(states)
    lane = iota((1, LANES), 1).astype(F32)

    def place(k, carry):
        row = pl.ds(lax.shift_right_logical(cell_ref[0, k], 7), 1)
        source = pl.ds(k, 1)
        mask = lanes[source, :] == lane
        pltpu.store(kinds.at[row, :], kind_cols[source, :], mask=mask)
        pltpu.store(states.at[row, :], state_cols[source, :], mask=mask)
        return carry

    lax.fori_loop(0, nodes, place, 0, unroll=32)


def stencil(start, last, pole_ref, loss_ref, below, here_ref, above, previous, speed, kinds,
            states, *outs):
    copies = len(outs) in (3, 6)
    out, states_out = outs[-3:-1] if copies else outs[-2:]
    _, rows, nz = previous.shape
    groups, chunks = nz // LANES, rows // 8
    x = start + pl.program_id(0)
    lane, sub = iota((8, LANES), 1), iota((8, LANES), 0)
    first_lane, last_lane = lane == 0, lane == LANES - 1
    first_sub, last_sub = sub == 0, sub == 7
    pole = jnp.zeros((8, LANES), F32)
    gain = jnp.zeros((8, LANES), F32)
    for at in range(pole_ref.shape[0]):
        pole = jnp.where(lane == at + 1, pole_ref[at], pole)
        gain = jnp.where(lane == at + 1, loss_ref[at] * (1.0 - pole_ref[at]), gain)
    has_below = jnp.where(x > 0, 1.0, 0.0)
    has_above = jnp.where(x < last, 1.0, 0.0)

    def tile(ref, j, g):
        return ref[0, 8 * j : 8 * j + 8, LANES * g : LANES * (g + 1)]

    def row_tiles(j):
        tiles = [tile(here_ref, j, g) for g in range(groups)]
        return tiles, [pltpu.roll(t, 1, 0) for t in tiles], [pltpu.roll(t, 7, 0) for t in tiles]

    zero = jnp.zeros((8, LANES), F32)
    blank = [zero] * groups
    behind, current = (blank,) * 3, row_tiles(0)
    for j in range(chunks):
        ahead = row_tiles(j + 1) if j + 1 < chunks else (blank,) * 3
        heres, downs, ups = current
        lefts = [zero] + [pltpu.roll(t, 1, 1) for t in heres]
        rights = [pltpu.roll(t, LANES - 1, 1) for t in heres] + [zero]
        for g in range(groups):
            here = heres[g]
            left = jnp.where(first_lane, lefts[g], lefts[g + 1])
            right = jnp.where(last_lane, rights[g + 1], rights[g])
            up = jnp.where(first_sub, behind[1][g], downs[g])
            down = jnp.where(last_sub, ahead[2][g], ups[g])
            beside = has_below * tile(below, j, g) + has_above * tile(above, j, g)
            beside = beside + up + down + left + right
            value = 2.0 * here - tile(previous, j, g)
            value = value + tile(speed, j, g).astype(F32) * (beside - 6.0 * here)
            at = pl.ds(8 * j * groups + g, 8, stride=groups)
            kind = kinds[at, :].astype(jnp.int32)
            state = jnp.take_along_axis(pole, kind, axis=1) * states[at, :]
            state = state + jnp.take_along_axis(gain, kind, axis=1) * value
            states_out[at, :] = state
            out[0, 8 * j : 8 * j + 8, LANES * g : LANES * (g + 1)] = value - state
            if copies:
                outs[-1][0, 8 * j : 8 * j + 8, LANES * g : LANES * (g + 1)] = here
        behind, current = current, ahead


def received(one, two, axis):
    at = lax.axis_index(axis)
    even = lax.rem(at, 2) == 0
    one, two = one[...].astype(F32), two[...].astype(F32)
    has_low = jnp.where(at > 0, 1.0, 0.0)
    has_high = jnp.where(at < lax.axis_size(axis) - 1, 1.0, 0.0)
    return has_low * jnp.where(even, two, one), has_high * jnp.where(even, one, two)


def paired(low, high, axis):
    even = lax.rem(lax.axis_index(axis), 2) == 0
    return jnp.where(even, high, low).astype(BF16), jnp.where(even, low, high).astype(BF16)


def edges(first, last, top, bottom, sx_one, sx_two, sy_one, sy_two):
    sx_one[...], sx_two[...] = paired(first[0], last[0], "gx")
    final = bottom.shape[1] - 1
    for x in range(top.shape[0]):
        line = slice(x, x + 1)
        sy_one[line, :], sy_two[line, :] = paired(
            top[x, 0:1, :], bottom[x, final : final + 1, :], "gy"
        )


def fix_planes(first, last, top, bottom, c_first, c_last, c_top, c_bottom, x_halo, y_halo):
    slab, rows = top.shape[0], first.shape[1]
    final = top.shape[1] - 1
    for at, value, speed, halo in (
        (0, first, c_first, x_halo[0]),
        (slab - 1, last, c_last, x_halo[1]),
    ):
        value[0] = value[0] + speed[0].astype(F32) * halo
        for row, beside in ((0, y_halo[0]), (rows - 1, y_halo[1])):
            one = slice(row, row + 1)
            term = speed[0, one, :].astype(F32) * beside[at : at + 1, :]
            value[0, one, :] = value[0, one, :] + term
    top[0], bottom[0] = first[0, :8, :], first[0, rows - 8 :, :]
    top[slab - 1], bottom[slab - 1] = last[0, :8, :], last[0, rows - 8 :, :]
    for x in range(1, slab - 1):
        term = c_top[x, 0:1, :].astype(F32) * y_halo[0][x : x + 1, :]
        top[x, 0:1, :] = top[x, 0:1, :] + term
        term = c_bottom[x, 15:16, :].astype(F32) * y_halo[1][x : x + 1, :]
        bottom[x, final : final + 1, :] = bottom[x, final : final + 1, :] + term


def fix_and_send(field_in, c_first, c_last, c_top, c_bottom, x_one, x_two, y_one, y_two,
                 field, sx_one, sx_two, sy_one, sy_two, first, last, top, bottom, sems):
    slab, rows = top.shape[0], first.shape[1]
    places = (
        (pl.ds(0, 1), pl.ds(0, rows), first),
        (pl.ds(slab - 1, 1), pl.ds(0, rows), last),
        (pl.ds(0, slab), pl.ds(0, 8), top),
        (pl.ds(0, slab), pl.ds(rows - 8, 8), bottom),
    )
    copies = [
        pltpu.make_async_copy(field_in.at[x, y], ref, sems.at[at])
        for at, (x, y, ref) in enumerate(places)
    ]
    for copy in copies:
        copy.start()
    for copy in copies:
        copy.wait()
    fix_planes(first, last, top, bottom, c_first, c_last, c_top, c_bottom,
               received(x_one, x_two, "gx"), received(y_one, y_two, "gy"))
    copies = [
        pltpu.make_async_copy(ref, field.at[x, y], sems.at[at])
        for at, (x, y, ref) in enumerate(places[:2])
    ]
    inner = pl.ds(1, slab - 2)
    copies += [
        pltpu.make_async_copy(ref.at[inner], field.at[inner, y], sems.at[at + 2])
        for at, (_, y, ref) in enumerate(places[2:])
    ]
    for copy in copies:
        copy.start()
    edges(first, last, top, bottom, sx_one, sx_two, sy_one, sy_two)
    for copy in copies:
        copy.wait()


def gather_nodes(cell_ref, loss_ref, states, cells, material, order, filter_out, picked):
    nodes = cells.shape[1]

    def pick(k, carry):
        row = lax.shift_right_logical(cell_ref[0, k], 7)
        picked[pl.ds(k, 1), :] = states[pl.ds(row, 1), :]
        return carry

    lax.fori_loop(0, nodes, pick, 0, unroll=32)
    lane_row = (cells[...] & (LANES - 1)).astype(F32)
    inverse = 1.0 / lookup(material[...], loss_ref, 0)
    lane = iota((GROUP, LANES), 1).astype(F32)
    ones = jnp.ones((8, LANES), BF16)
    for at in range(nodes // GROUP):
        part = slice(at * GROUP, (at + 1) * GROUP)
        rest = jnp.where(columns_small(lane_row[:, part]) == lane, picked[part, :], 0.0)
        line = jnp.zeros((8, GROUP), F32)
        for _ in range(2):
            piece = rest.astype(BF16)
            rest = rest - piece.astype(F32)
            line = line + lax.dot_general(
                ones, piece, (((1,), (1,)), ((), ())), preferred_element_type=F32
            )
        filter_out[:, part] = line[0:1, :] * inverse[:, part]


def finish(anchor_ref, pressure_in, c_first, c_last, c_top, c_bottom, x_one, x_two, y_one, y_two,
           pairs_in, axial_in, mix_in, pressure_out, partial,
           pressure, pairs, axial, mix, planar, products_low, products_high, sems):
    slab, rows, nz = pressure.shape
    spheres = partial.shape[0]
    count = pairs.shape[0] // 2
    incoming = [
        pltpu.make_async_copy(source, target, sems.at[at])
        for at, (source, target) in enumerate((
            (pressure_in, pressure), (pairs_in, pairs), (axial_in, axial), (mix_in, mix),
        ))
    ]
    for copy in incoming:
        copy.start()
    products = (products_low, products_high)
    products_high[...] = jnp.zeros_like(products_high)
    incoming[0].wait()
    x_first = lax.axis_index("gx") * slab
    y_first = lax.axis_index("gy") * rows
    s_first = lax.axis_index("gy") * spheres
    x_halo, y_halo = received(x_one, x_two, "gx"), received(y_one, y_two, "gy")
    for at, speed, halo in ((0, c_first, x_halo[0]), (slab - 1, c_last, x_halo[1])):
        pressure[at] = pressure[at] + speed[0].astype(F32) * halo
    for x in range(slab):
        for row, speed, r, halo in ((0, c_top, 0, y_halo[0]), (rows - 1, c_bottom, 15, y_halo[1])):
            one = slice(row, row + 1)
            term = speed[x, r : r + 1, :].astype(F32) * halo[x : x + 1, :]
            pressure[x, one, :] = pressure[x, one, :] + term
    outgoing = pltpu.make_async_copy(pressure, pressure_out, sems.at[0])
    outgoing.start()
    for copy in incoming[1:]:
        copy.wait()
    limit = CUBE * CUBE
    odd_y = 2 * iota((CUBE, 2 * LANES), 0) - (CUBE - 1)
    y_square = odd_y * odd_y
    lane = iota((CUBE, 2 * LANES), 1)

    def across(s, carry):
        x0 = anchor_ref[0, s_first + s]
        y0 = pl.multiple_of(anchor_ref[1, s_first + s] - y_first, CUBE)
        z0 = anchor_ref[2, s_first + s]
        start = pl.multiple_of(window_start(z0, nz), LANES)
        odd_z = 2 * (lane - (z0 - start)) - (CUBE - 1)
        square = y_square + odd_z * odd_z
        a0 = x_first - x0
        planes = []
        for i in range(slab):
            odd_x = 2 * (a0 + i) - (CUBE - 1)
            values = pressure[i, pl.ds(y0, CUBE), pl.ds(start, 2 * LANES)]
            planes.append(jnp.where(square <= limit - odd_x * odd_x, values, 0.0).astype(BF16))
        blank = jnp.zeros((LANES - 2 * CUBE, 2 * LANES), BF16)
        first = jnp.clip(a0, -slab, CUBE) + slab
        left, right = [], []
        for i in range(0, slab, 2):
            at = pl.multiple_of(jnp.minimum(first + i, CUBE + 2 * slab - 1) * LANES, LANES)
            left.append(pairs[:, pl.ds(at, LANES)])
            right += [planes[i], planes[i + 1], blank]
        total = dot(jnp.concatenate(left, axis=1), jnp.concatenate(right, axis=0))
        planar[s] = total[:count] + total[count:]
        return carry

    def along(s, carry):
        high, low = split(planar[s])
        factor = axial[lax.shift_right_logical(anchor_ref[2, s_first + s] * 1366, 16)]
        contract = (((1,), (1,)), ((), ()))
        one = lax.dot_general(factor, high, contract, preferred_element_type=F32)
        two = lax.dot_general(factor[:DEGREES], low, contract, preferred_element_type=F32)
        moment = one[:DEGREES] + one[DEGREES:] + two
        at = pl.ds(pl.multiple_of(s * DEGREES, DEGREES), DEGREES)
        products[0][at, :] = moment[:, :LANES]
        products[1][at, 0 : count - LANES] = moment[:, LANES:]
        return carry

    lax.fori_loop(0, spheres, across, 0, unroll=16)
    lax.fori_loop(0, spheres, along, 0, unroll=32)
    result = jnp.zeros((spheres, COEFS), F32)
    for q in range(DEGREES):
        at = pl.ds(q, spheres, stride=DEGREES)
        moment = jnp.concatenate([products[0][at, :], products[1][at, :]], axis=1)
        first, size = mix_rows(q)
        high, low = split(moment[:, :size])
        upper, lower = mix[0, first : first + size], mix[1, first : first + size]
        result = result + (dot(high, upper) + (dot(low, upper) + dot(high, lower)))
    partial[...] = result
    outgoing.wait()


def whole(memory=pltpu.VMEM):
    return pl.BlockSpec(memory_space=memory)


def after(value, *others):
    return lax.optimization_barrier((value, *others))


def shards(now, prev, speed, node_cell, node_material, filter_state, pole, loss, anchors):
    slab, rows, nz = now.shape
    nodes = node_cell.shape[-1]
    spheres = anchors.shape[0] // lax.axis_size("gy")
    per_plane = rows * nz // LANES
    cells = node_cell.reshape(1, nodes)
    material = node_material.reshape(1, nodes)
    state = filter_state.reshape(1, nodes)
    dense = jax.ShapeDtypeStruct((slab * per_plane, LANES), F32)
    block = jax.ShapeDtypeStruct((slab, rows, nz), F32)
    sends = (jax.ShapeDtypeStruct((rows, nz), BF16),) * 2
    sends += (jax.ShapeDtypeStruct((slab, nz), BF16),) * 2
    smem = whole(pltpu.SMEM)

    def params(mebibytes):
        return pltpu.CompilerParams(vmem_limit_bytes=mebibytes << 20)

    def swap(value, axis, side):
        count = lax.axis_size(axis)
        moves = [1 - 2 * (i % 2) if side == 0 else 2 * (i % 2) - 1 for i in range(count)]
        return lax.ppermute(value, axis, [(i, (i + moves[i]) % count) for i in range(count)])

    def plane_at(x):
        return pl.BlockSpec((1, rows, nz), lambda i: (x, 0, 0))

    def rows_at(y, height):
        return pl.BlockSpec((slab, height, nz), lambda i: (0, y // height, 0))

    speeds = [speed] * 4
    edge_specs = [plane_at(0), plane_at(slab - 1), rows_at(0, 16), rows_at(rows - 16, 16)]

    def step(centre, previous, kinds, states, part, limit, copies, done=()):
        start, stop = part

        def plane(move):
            return pl.BlockSpec(
                (1, rows, nz), lambda i: (jnp.clip(i + start + move, 0, slab - 1), 0, 0)
            )

        map_spec = pl.BlockSpec((per_plane, LANES), lambda i: (i + start, 0))
        return pl.pallas_call(
            functools.partial(stencil, start, slab - 1),
            grid=(stop - start,),
            out_shape=(block, dense) + (block,) * copies,
            in_specs=[smem] * 2 + [plane(-1), plane(0), plane(1), plane(0), plane(0)]
            + [map_spec] * 2 + [whole(pl.ANY)] * len(done),
            out_specs=(plane(0), map_spec) + (plane(0),) * copies,
            input_output_aliases={9 + at: at for at in range(len(done))},
            compiler_params=params(limit),
            name="stencil",
        )(pole, loss, centre, centre, centre, previous, speed, kinds, states, *done)

    layers = [pltpu.VMEM((1, rows, nz), F32)] * 2 + [pltpu.VMEM((slab, 8, nz), F32)] * 2
    layers += [pltpu.SemaphoreType.DMA((4,))]
    sx_one, sx_two, sy_one, sy_two = pl.pallas_call(
        edges,
        grid=(1,),
        out_shape=sends,
        in_specs=[plane_at(0), plane_at(slab - 1), rows_at(0, 8), rows_at(rows - 8, 8)],
        out_specs=(whole(),) * 4,
        compiler_params=params(16),
        name="edges",
    )(now, now, now, now)
    x_one, x_two = swap(sx_one, "gx", 0), swap(sx_two, "gx", 1)
    y_one, y_two = swap(sy_one, "gy", 0), swap(sy_two, "gy", 1)
    kinds, states = pl.pallas_call(
        node_maps,
        out_shape=(dense, dense),
        in_specs=[smem] * 2 + [whole()] * 3,
        out_specs=(whole(),) * 2,
        scratch_shapes=[pltpu.VMEM((nodes, LANES), F32)] * 3,
        compiler_params=params(16),
        name="node_maps",
    )(cells, loss, cells, material, state)
    (kinds,) = after(kinds)
    half, states = step(now, prev, kinds, states, (0, slab), 16, False)
    half, sx_one, sx_two, sy_one, sy_two = pl.pallas_call(
        fix_and_send,
        grid=(1,),
        out_shape=(block,) + sends,
        in_specs=[whole(pl.ANY)] + edge_specs + [whole()] * 4,
        out_specs=(whole(pl.ANY),) + (whole(),) * 4,
        scratch_shapes=layers,
        input_output_aliases={0: 0},
        compiler_params=params(16),
        name="fix_and_send",
    )(half, *speeds, x_one, x_two, y_one, y_two)
    x_one, x_two = swap(sx_one, "gx", 0), swap(sx_two, "gx", 1)
    first_part = step(half, now, kinds, states, (0, slab // 2), 16, True)
    sy_one, sy_two, *first_part = after(sy_one, sy_two, *first_part)
    y_one, y_two = swap(sy_one, "gy", 0), swap(sy_two, "gy", 1)
    partly, states, before = step(
        half, now, kinds, states, (slab // 2, slab), 16, True, first_part
    )
    fit_tables = (plane_pairs(slab), axial_windows(nz), mix_table())
    pressure, partial = pl.pallas_call(
        finish,
        grid=(1,),
        out_shape=(block, jax.ShapeDtypeStruct((spheres, COEFS), F32)),
        in_specs=[smem, whole(pl.ANY)] + edge_specs + [whole()] * 4 + [whole(pltpu.HBM)] * 3,
        out_specs=(whole(pl.ANY), whole()),
        scratch_shapes=[pltpu.VMEM(block.shape, F32)]
        + [pltpu.VMEM(table.shape, BF16) for table in fit_tables]
        + [
            pltpu.VMEM((spheres, fit_tables[0].shape[0] // 2, 2 * LANES), F32),
            pltpu.VMEM((spheres * DEGREES, LANES), F32),
            pltpu.VMEM((spheres * DEGREES, LANES), F32),
            pltpu.SemaphoreType.DMA((4,)),
        ],
        compiler_params=params(32),
        name="finish",
    )(
        anchors.T, partly, *speeds,
        x_one, x_two, y_one, y_two, *(jnp.asarray(table) for table in fit_tables),
    )
    eight = lax.axis_size("gx") == 8
    if eight:
        partial = partial + swap(partial, "gx", 0)
        others = [
            lax.ppermute(partial, "gx", [(i, i ^ move) for i in range(8)]) for move in (2, 4, 6)
        ]
        coefficients = (partial + others[0]) + (others[1] + others[2])
    else:
        coefficients = jnp.sum(lax.all_gather(partial, "gx", axis=0, tiled=False), axis=0)
    filter_out = pl.pallas_call(
        gather_nodes,
        out_shape=jax.ShapeDtypeStruct((1, nodes), F32),
        in_specs=[smem] * 2 + [whole()] * 3 + [whole(pl.ANY)],
        out_specs=whole(),
        scratch_shapes=[pltpu.VMEM((nodes, LANES), F32)],
        compiler_params=params(16),
        name="gather_nodes",
    )(cells, loss, states, cells, material, partial)
    return pressure, before, filter_out.reshape(filter_state.shape), coefficients


def solution(mesh):
    grid = P("gx", "gy", None)
    return jax.shard_map(
        shards,
        mesh=mesh,
        in_specs=(grid,) * 6 + (P(), P(), P()),
        out_specs=(grid, grid, grid, P("gy", None)),
        check_vma=False,
    )
```
